768 devices in a mesh: wide: 96 (over z, x, core), grp: 8 (over y).
Axes of the slice: x: 4, y: 8, z: 12, core: 2. Of those that a mesh axis runs over, the one named last changes fastest.
Arguments:
- state: float32 [5, 125, 98304], P(None, None, ('wide', 'grp')), as said below
- metric: float32 [98304], P(('wide', 'grp')), may hold values from 1 to 4
- nbr_elem: int32 [6, 98304], P(None, ('wide', 'grp')), may hold values from 0 to 98303, as said below
- nbr_face: int32 [6, 98304], P(None, ('wide', 'grp')), may hold values from 0 to 5, as said below
- troubled: int32 [36864], P(('wide', 'grp')), may hold values from -1 to 127, as said below
- new_owner: int32 [98304], P(('wide', 'grp')), may hold values from 0 to 767, as said below
Outputs:
- migrated: float32 [5, 125, 147456], P(None, None, ('wide', 'grp'))
The draws below stay inside these ranges and needn't reach their ends.
Inputs may be any that keep to these rules, and one draw needn't show every extreme that they name: Across face f of element e lies face nbr_face[f, e] of element nbr_elem[f, e], and that face lies across face f of element e again; a face never meets itself. The element across lies on the same device, or on another device of the same grp group, exactly 16 faces with each of them, or on a wide neighbour (same grp index, wide index minus or plus one, wrapping), exactly 32 faces with each of the two. `nbr_face`: see nbr_elem. `troubled`: each device's 48 entries list distinct local element indices first and -1 after them; every draw has devices whose list is full. `new_owner`: each element's new owner is its device or one of its two wide neighbours; at most 32 elements of a device go to each neighbour, and every draw has devices that send 32 to both. `state`: at every node density and pressure lie between 0.4 and 2.5 and each velocity component within -0.9 to 0.9.
All inputs are finite; a program needn't handle non-finite values.
Results may differ from the reference program's by a relative error of at most 0.0001.
Values sent between devices are 32-bit elements; how exact they have to be, the bound alone decides.
No kernel may reach another device: no remote copies, remote signals or barrier semaphores. Data moves between devices by JAX's collectives and lax.ppermute only.
A program may use at most 32 MiB of HBM per device.

```python
import math
import jax
import jax.numpy as jnp
import numpy as np
from jax import lax

ELEM_NODES = 125
ELEM_DEV = 128
GROUP_FACES = 16
WIDE_FACES = 32
TROUBLE_CAP = 48
MOVE_CAP = 32
ELEMS = 98304
N_WIDE = 96
N_GRP = 8


def connectivity(key):
    devices = N_WIDE * N_GRP
    slot_count = 6 * ELEM_DEV
    key_list = jax.random.split(jax.random.fold_in(key, 11), devices)
    perms = jax.vmap(lambda k: jax.random.permutation(k, slot_count))(key_list).astype(jnp.int32)
    device_ids = jnp.arange(devices, dtype=jnp.int32)[:, None]
    position = jnp.arange(slot_count, dtype=jnp.int32)[None, :]
    wide_pos = device_ids // N_GRP
    group_pos = device_ids % N_GRP
    group_total = (N_GRP - 1) * GROUP_FACES
    block = position // GROUP_FACES
    within = position % GROUP_FACES
    peer_group = (group_pos + block + 1) % N_GRP
    group_device = wide_pos * N_GRP + peer_group
    group_back = (N_GRP - 2 - block) * GROUP_FACES + within
    left_device = (wide_pos - 1) % N_WIDE * N_GRP + group_pos
    left_back = group_total + WIDE_FACES + (position - group_total)
    right_device = (wide_pos + 1) % N_WIDE * N_GRP + group_pos
    right_back = group_total + (position - group_total - WIDE_FACES)
    base_pos = group_total + 2 * WIDE_FACES
    inner_back = base_pos + jnp.bitwise_xor(position - base_pos, 1)
    in_group = position < group_total
    in_left = (position >= group_total) & (position < group_total + WIDE_FACES)
    in_right = (position >= group_total + WIDE_FACES) & (position < base_pos)
    partner_device = jnp.where(in_group, group_device, jnp.where(in_left, left_device, jnp.where(in_right, right_device, device_ids + 0 * position)))
    partner_pos = jnp.where(in_group, group_back, jnp.where(in_left, left_back, jnp.where(in_right, right_back, inner_back)))
    partner_slot = perms[partner_device, partner_pos]
    partner_elem = partner_device * ELEM_DEV + partner_slot % ELEM_DEV
    partner_face = partner_slot // ELEM_DEV
    inverse = jnp.argsort(perms, axis=1, stable=True)
    elem_by_slot = jnp.take_along_axis(partner_elem, inverse, axis=1)
    face_by_slot = jnp.take_along_axis(partner_face, inverse, axis=1)
    elem_out = jnp.transpose(elem_by_slot.reshape(devices, 6, ELEM_DEV), (1, 0, 2)).reshape(6, ELEMS)
    face_output = jnp.transpose(face_by_slot.reshape(devices, 6, ELEM_DEV), (1, 0, 2)).reshape(6, ELEMS)
    return (elem_out.astype(jnp.int32), face_output.astype(jnp.int32))


def draw_nbr_elem(key, part):
    return connectivity(key)[0]


def draw_nbr_face(key, part):
    return connectivity(key)[1]


def draw_troubled(key, part):
    devices = N_WIDE * N_GRP
    key_list = jax.random.split(jax.random.fold_in(key, 23), devices + 1)
    counts = jax.random.randint(key_list[devices], (devices,), TROUBLE_CAP // 4, TROUBLE_CAP + 1)
    group_pos = jnp.arange(devices, dtype=jnp.int32) % N_GRP
    counts = jnp.where(group_pos == 0, TROUBLE_CAP, counts)
    perms = jax.vmap(lambda k: jax.random.permutation(k, ELEM_DEV))(key_list[:devices]).astype(jnp.int32)
    listed = perms[:, :TROUBLE_CAP]
    filled = jnp.arange(TROUBLE_CAP, dtype=jnp.int32)[None, :] < counts[:, None]
    return jnp.where(filled, listed, -1).reshape(-1).astype(jnp.int32)


def draw_new_owner(key, part):
    devices = N_WIDE * N_GRP
    key_list = jax.random.split(jax.random.fold_in(key, 37), devices + 2)
    group_pos = jnp.arange(devices, dtype=jnp.int32) % N_GRP
    wide_pos = jnp.arange(devices, dtype=jnp.int32) // N_GRP
    count_left = jax.random.randint(key_list[devices], (devices,), MOVE_CAP // 4, MOVE_CAP + 1)
    count_right = jax.random.randint(key_list[devices + 1], (devices,), MOVE_CAP // 4, MOVE_CAP + 1)
    count_left = jnp.where(group_pos == 0, MOVE_CAP, count_left)
    count_right = jnp.where(group_pos == 0, MOVE_CAP, count_right)
    perms = jax.vmap(lambda k: jax.random.permutation(k, ELEM_DEV))(key_list[:devices]).astype(jnp.int32)
    ranks = jnp.argsort(perms, axis=1, stable=True)
    own_device = (wide_pos * N_GRP + group_pos)[:, None]
    left_device = ((wide_pos - 1) % N_WIDE * N_GRP + group_pos)[:, None]
    right_device = ((wide_pos + 1) % N_WIDE * N_GRP + group_pos)[:, None]
    owner = jnp.where(ranks < count_left[:, None], left_device, jnp.where(ranks < (count_left + count_right)[:, None], right_device, own_device))
    return owner.reshape(-1).astype(jnp.int32)


def draw_state(key, part):
    key_list = jax.random.split(jax.random.fold_in(key, 3), 5)
    grid_shape = (ELEM_NODES, ELEMS)
    low = math.log(0.5)
    high = math.log(2.0)
    density = jnp.exp(jax.random.uniform(key_list[0], grid_shape, minval=low, maxval=high))
    velocity_x = jax.random.uniform(key_list[1], grid_shape, minval=-0.5, maxval=0.5)
    velocity_y = jax.random.uniform(key_list[2], grid_shape, minval=-0.5, maxval=0.5)
    velocity_z = jax.random.uniform(key_list[3], grid_shape, minval=-0.5, maxval=0.5)
    pressure = jnp.exp(jax.random.uniform(key_list[4], grid_shape, minval=low, maxval=high))
    speed_sq = velocity_x * velocity_x + velocity_y * velocity_y + velocity_z * velocity_z
    energy = pressure / 0.4 + 0.5 * density * speed_sq
    stacked = jnp.stack([density, density * velocity_x, density * velocity_y, density * velocity_z, energy])
    return stacked.astype(jnp.float32)


def levels(key, extent, pieces, smallest, largest):
    level, own = 1.0, jax.random.fold_in(key, 6)
    for dim, shards_of in pieces:
        steps = jnp.exp(jax.random.uniform(jax.random.fold_in(own, dim), (shards_of,), jnp.float32, smallest / len(pieces), largest / len(pieces)))
        level = level * jnp.repeat(steps, extent[dim] // shards_of).reshape([-1 if axis == dim else 1 for axis in range(len(extent))])
    return level


def setup_inputs(seed: int = 0) -> dict:
    seeds = jax.random.split(jax.random.key(seed), 7)
    return {
        "state": draw_state(jax.random.fold_in(seeds[6], 71), 0),
        "metric": jnp.clip(jnp.exp(math.log(4.0) - 1.3862944 * jax.random.uniform(seeds[1], (ELEMS,), jnp.float32) ** levels(seeds[1], (ELEMS,), ((0, 768),), -0.2, 0.2)), 1.0, 4.0),
        "nbr_elem": draw_nbr_elem(jax.random.fold_in(seeds[6], 71), 0),
        "nbr_face": draw_nbr_face(jax.random.fold_in(seeds[6], 71), 0),
        "troubled": draw_troubled(jax.random.fold_in(seeds[6], 71), 0),
        "new_owner": draw_new_owner(jax.random.fold_in(seeds[6], 71), 0),
    }


SECTION_STEP = 0.01
LIFT_GAIN = 10.0

def gll_tables():
    root = math.sqrt(3.0 / 7.0)
    points = np.array([-1.0, -root, 0.0, root, 1.0])
    weights = np.array([0.1, 49.0 / 90.0, 32.0 / 45.0, 49.0 / 90.0, 0.1])
    bary = np.array([1.0 / np.prod([points[j] - points[k] for k in range(5) if k != j]) for j in range(5)])
    deriv = np.zeros((5, 5))
    for i in range(5):
        for j in range(5):
            if i != j:
                deriv[i, j] = bary[j] / bary[i] / (points[i] - points[j])
        deriv[i, i] = -np.sum(deriv[i])
    ident = np.eye(5)
    diffs = [np.kron(np.kron(deriv, ident), ident), np.kron(np.kron(ident, deriv), ident), np.kron(np.kron(ident, ident), deriv)]
    cell_weights = np.kron(np.kron(weights, weights), weights) / 8.0
    face_table = np.zeros((6, 25), np.int32)
    for a in range(5):
        for b in range(5):
            face_table[0, 5 * a + b] = 5 * a + b
            face_table[1, 5 * a + b] = 100 + 5 * a + b
            face_table[2, 5 * a + b] = 25 * a + b
            face_table[3, 5 * a + b] = 25 * a + 20 + b
            face_table[4, 5 * a + b] = 25 * a + 5 * b
            face_table[5, 5 * a + b] = 25 * a + 5 * b + 4
    return (diffs, cell_weights, face_table)

def pressure_of(u):
    density = u[0]
    return 0.4 * (u[4] - 0.5 * (u[1] * u[1] + u[2] * u[2] + u[3] * u[3]) / density)

def inviscid_flux(u, axis_label):
    density = u[0]
    velocity = u[1 + axis_label] / density
    pressure = pressure_of(u)
    rows = [u[1 + axis_label], u[1] * velocity, u[2] * velocity, u[3] * velocity, (u[4] + pressure) * velocity]
    rows[1 + axis_label] = rows[1 + axis_label] + pressure
    return jnp.stack(rows)

def signal_speed(u, axis_label):
    density = u[0]
    return jnp.abs(u[1 + axis_label] / density) + jnp.sqrt(1.4 * pressure_of(u) / density)

def section_update(state, metric, neighbour_traces):
    diffs, cell_weights, face_table = gll_tables()
    volume_term = jnp.zeros_like(state)
    for axis_label in range(3):
        operator_matrix = jnp.asarray(diffs[axis_label], state.dtype)
        volume_term = volume_term + jnp.einsum('lk,bkr->blr', operator_matrix, inviscid_flux(state, axis_label), precision=lax.Precision.HIGHEST)
    change = -metric[None, None, :] * volume_term
    for face in range(6):
        axis_label = face // 2
        sign_value = -1.0 if face % 2 == 0 else 1.0
        inner = state[:, face_table[face], :]
        outer = neighbour_traces[face]
        flux_in = sign_value * inviscid_flux(inner, axis_label)
        flux_out = sign_value * inviscid_flux(outer, axis_label)
        speed = jnp.maximum(signal_speed(inner, axis_label), signal_speed(outer, axis_label))
        common = 0.5 * (flux_in + flux_out) - 0.5 * speed[None] * (outer - inner)
        lift = (LIFT_GAIN * metric)[None, None, :] * (flux_in - common)
        change = change.at[:, face_table[face], :].add(lift)
    return state + SECTION_STEP * change

def cell_mean(values, cell_weights):
    return lax.optimization_barrier(jnp.sum(values * cell_weights[None, :, None], axis=1))

def weno_combine(own, neighbours, cell_weights):
    own_mean = cell_mean(own, cell_weights)
    candidates = [(own, 0.4)]
    for other in neighbours:
        candidates.append((other - cell_mean(other, cell_weights)[:, None, :] + own_mean[:, None, :], 0.1))
    numer = jnp.zeros_like(own)
    denom = jnp.zeros_like(own_mean)
    for values, linear in candidates:
        spread = values - cell_mean(values, cell_weights)[:, None, :]
        smooth = lax.optimization_barrier(jnp.sum(cell_weights[None, :, None] * spread * spread, axis=1))
        weight = linear / ((1e-06 + smooth) * (1e-06 + smooth))
        numer = numer + weight[:, None, :] * values
        denom = denom + weight
    return numer / denom[:, None, :]

def reference(state, metric, nbr_elem, nbr_face, troubled, new_owner):
    diffs, cell_weights_np, face_table = gll_tables()
    cell_weights = jnp.asarray(cell_weights_np, state.dtype)
    elem_total = state.shape[2]
    devices = N_WIDE * N_GRP
    traces = state[:, face_table, :]
    flat = jnp.transpose(traces, (0, 2, 1, 3)).reshape(5, 25, 6 * elem_total)
    neighbour = [flat[:, :, nbr_face[face] * elem_total + nbr_elem[face]] for face in range(6)]
    sectioned = section_update(state, metric, neighbour)
    listed = troubled.reshape(devices, TROUBLE_CAP)
    valid = listed >= 0
    offsets = (jnp.arange(devices, dtype=jnp.int32) * ELEM_DEV)[:, None]
    global_ids = jnp.where(valid, listed + offsets, 0).reshape(-1).astype(jnp.int32)
    own = sectioned[:, :, global_ids]
    neighbours = [sectioned[:, :, nbr_elem[face, global_ids]] for face in range(6)]
    limited_cells = weno_combine(own, neighbours, cell_weights)
    target = jnp.where(valid.reshape(-1), global_ids, elem_total).astype(jnp.int32)
    limited = sectioned.at[:, :, target].set(limited_cells, mode='drop')
    elem_ids = jnp.arange(elem_total, dtype=jnp.int32)
    source = elem_ids // ELEM_DEV
    local = elem_ids % ELEM_DEV
    source_wide = source // N_GRP
    source_group = source % N_GRP
    left_device = (source_wide - 1) % N_WIDE * N_GRP + source_group
    right_device = (source_wide + 1) % N_WIDE * N_GRP + source_group
    goes_left = new_owner == left_device
    goes_right = new_owner == right_device
    stays = new_owner == source
    rank_left = (jnp.cumsum(goes_left.reshape(devices, ELEM_DEV).astype(jnp.int32), axis=1, dtype=jnp.int32) - 1).reshape(-1)
    rank_right = (jnp.cumsum(goes_right.reshape(devices, ELEM_DEV).astype(jnp.int32), axis=1, dtype=jnp.int32) - 1).reshape(-1)
    slot_capacity = ELEM_DEV + 2 * MOVE_CAP
    slot = jnp.where(stays, source * slot_capacity + local, jnp.where(goes_right, new_owner * slot_capacity + ELEM_DEV + rank_right, new_owner * slot_capacity + ELEM_DEV + MOVE_CAP + rank_left)).astype(jnp.int32)
    migrated = jnp.zeros((5, 125, devices * slot_capacity), jnp.float32).at[:, :, slot].set(limited)
    return migrated
```

```python
import functools
import math

import jax
import jax.numpy as jnp
import numpy as np
from jax import lax
from jax.experimental import pallas as pl
from jax.experimental.pallas import tpu as pltpu
from jax.sharding import PartitionSpec as P

GROUP_FACES = 16
WIDE_FACES = 32
MOVE_CAP = 32
SECTION_STEP = 0.01
LIFT_GAIN = 10.0

ELEM = 128
VARS = 5
NODES = 125
FACES = 6
GROUP = 8
GROUP_ROWS = GROUP * GROUP_FACES
PAIR0 = GROUP_ROWS
PAIR1 = GROUP_ROWS + WIDE_FACES
ROWS = GROUP_ROWS + 2 * WIDE_FACES
LOCAL = 10

F32 = jnp.float32
BF16 = jnp.bfloat16
I32 = jnp.int32
INTERPRET = False


def gll_tables():
    root = math.sqrt(3.0 / 7.0)
    points = np.array([-1.0, -root, 0.0, root, 1.0])
    weights = np.array([0.1, 49.0 / 90.0, 32.0 / 45.0, 49.0 / 90.0, 0.1])
    bary = np.array(
        [1.0 / np.prod([points[j] - points[k] for k in range(5) if k != j]) for j in range(5)]
    )
    deriv = np.zeros((5, 5))
    for i in range(5):
        for j in range(5):
            if i != j:
                deriv[i, j] = bary[j] / bary[i] / (points[i] - points[j])
        deriv[i, i] = -np.sum(deriv[i])
    ident = np.eye(5)
    diffs = [
        np.kron(np.kron(deriv, ident), ident),
        np.kron(np.kron(ident, deriv), ident),
        np.kron(np.kron(ident, ident), deriv),
    ]
    cell_weights = np.kron(np.kron(weights, weights), weights) / 8.0
    return diffs, cell_weights


def face_rows(face):
    if face < 2:
        return [(100 * face, 25, 1, 0)]
    if face < 4:
        return [(25 * a + 20 * (face - 2), 5, 1, 5 * a) for a in range(5)]
    return [(4 * (face - 4), 25, 5, 0)]


def rows_at(first, count, stride):
    return pl.ds(first, count) if stride == 1 else pl.ds(first, count, stride=stride)


def thirds(x):
    hi = x.astype(BF16)
    rest = x - hi.astype(F32)
    mid = rest.astype(BF16)
    lo = (rest - mid.astype(F32)).astype(BF16)
    return hi, mid, lo


def dot_nn(a, b):
    return lax.dot_general(a, b, (((1,), (0,)), ((), ())), preferred_element_type=F32)


def dot_nt(a, b):
    return lax.dot_general(a, b, (((1,), (1,)), ((), ())), preferred_element_type=F32)


def select_nt(onehot, values):
    hi, mid, lo = thirds(values)
    return dot_nt(onehot, hi) + dot_nt(onehot, mid) + dot_nt(onehot, lo)


def iota(shape, dim):
    return lax.broadcasted_iota(I32, shape, dim)


def onehot(mask):
    return jnp.where(mask, 1.0, 0.0).astype(BF16)


def places():
    wide = lax.axis_index("wide")
    grp = lax.axis_index("grp")
    size = lax.axis_size("wide")
    left = lax.rem(wide + size - 1, size) * GROUP + grp
    right = lax.rem(wide + 1, size) * GROUP + grp
    odd = lax.rem(wide, 2)
    return wide, grp, left, right, odd


def categories(nbr_elem):
    wide, grp, left, _, odd = places()
    owner = lax.shift_right_logical(nbr_elem, 7)
    beside = jnp.where(owner == left, 9 - odd, 8 + odd)
    cat = jnp.where(lax.shift_right_logical(owner, 3) == wide, owner & 7, beside)
    return jnp.where(owner == wide * GROUP + grp, LOCAL, cat)


def strict_upper():
    return onehot(iota((ELEM, ELEM), 0) < iota((ELEM, ELEM), 1))


def pack_kernel(elem_ref, state_ref, grp_ref, pair0_ref, pair1_ref, trace_ref, pick_ref, s_ref):
    cat = categories(elem_ref[...])
    kinds = iota((16, ELEM), 0)
    hot = [jnp.where(cat[f : f + 1, :] == kinds, 1.0, 0.0) for f in range(FACES)]
    upper = jnp.concatenate([strict_upper(), jnp.ones((ELEM, ELEM), BF16)], axis=1)
    counts = dot_nn(jnp.concatenate(hot, axis=0).astype(BF16), upper)
    base = jnp.where(kinds < 9, 16 * kinds, PAIR1).astype(F32)
    pick = jnp.zeros((ROWS, ELEM), F32)
    rows = iota((ROWS, ELEM), 0)
    for f in range(FACES):
        part = counts[16 * f : 16 * f + 16]
        pos = jnp.sum(hot[f] * (part[:, :ELEM] + base), axis=0, keepdims=True)
        base = base + part[:, ELEM:]
        pos = jnp.where(cat[f : f + 1, :] == LOCAL, -1, pos.astype(I32))
        chosen = jnp.where(rows == pos, 1.0, 0.0)
        pick = pick + chosen
        s_ref[:, f * ELEM : (f + 1) * ELEM] = chosen.astype(BF16)
    pick_ref[...] = pick.astype(BF16)
    for f in range(FACES):
        for v in range(VARS):
            for first, count, stride, place in face_rows(f):
                trace_ref[25 * v + place : 25 * v + place + count, f * ELEM : (f + 1) * ELEM] = state_ref[
                    v, rows_at(first, count, stride), :
                ]
    trace_ref[125:128, :] = jnp.zeros((3, FACES * ELEM), F32)
    sent = select_nt(s_ref[...], trace_ref[...])
    grp_ref[...] = sent[:GROUP_ROWS]
    pair0_ref[...] = sent[PAIR0:PAIR1]
    pair1_ref[...] = sent[PAIR1:]


def primitives(u):
    inv = 1.0 / u[0]
    vel = [u[1] * inv, u[2] * inv, u[3] * inv]
    kinetic = u[1] * vel[0] + u[2] * vel[1] + u[3] * vel[2]
    pressure = 0.4 * (u[4] - 0.5 * kinetic)
    return inv, vel, pressure


def flux(u, vel, pressure, a):
    w = vel[a]
    rows = [u[1 + a], u[1] * w, u[2] * w, u[3] * w, (u[4] + pressure) * w]
    rows[1 + a] = rows[1 + a] + pressure
    return rows


def speed(inv, vel, pressure, a):
    return jnp.abs(vel[a]) + jnp.sqrt(1.4 * pressure * inv)


def face_values(ref, f):
    return [ref[25 * v : 25 * v + 25, f * ELEM : (f + 1) * ELEM] for v in range(VARS)]


def add_face(ref, f, v, value):
    for first, count, stride, place in face_rows(f):
        at = rows_at(first, count, stride)
        ref[v, at, :] = ref[v, at, :] + value[place : place + count]


def local_kernel(
    elem_ref, face_ref, state_ref, metric_ref, trace_ref, diff_ref,
    base_ref, speed_ref, near_ref, take_ref, pos_ref, f_ref, key_ref,
):
    metric = metric_ref[...]
    u = [state_ref[v] for v in range(VARS)]
    inv, vel, pressure = primitives(u)
    for a in range(3):
        for v, row in enumerate(flux(u, vel, pressure, a)):
            f_ref[128 * a : 128 * a + NODES, v * ELEM : (v + 1) * ELEM] = row
        f_ref[128 * a + NODES : 128 * a + 128, :] = jnp.zeros((3, VARS * ELEM), F32)
    volume = jnp.dot(diff_ref[...], f_ref[...], precision=lax.Precision.HIGHEST, preferred_element_type=F32)
    for v in range(VARS):
        base_ref[v] = u[v] - (SECTION_STEP * metric) * volume[:NODES, v * ELEM : (v + 1) * ELEM]
    half = (0.5 * LIFT_GAIN * SECTION_STEP) * metric
    for f in range(FACES):
        a = f // 2
        scale = half if f % 2 else -half
        inner = face_values(trace_ref, f)
        inv, vel, pressure = primitives(inner)
        speed_ref[f] = speed(inv, vel, pressure, a)
        for v, row in enumerate(flux(inner, vel, pressure, a)):
            add_face(base_ref, f, v, scale * row)
    cat = categories(elem_ref[...])
    partner = face_ref[...] * ELEM + (elem_ref[...] & (ELEM - 1))
    _, grp, _, _, _ = places()
    key = jnp.concatenate([cat * (FACES * ELEM) + partner, jnp.zeros((2, ELEM), I32)], axis=0)
    key_ref[...] = key.astype(F32).T
    keys = key.astype(F32)
    rank = [jnp.zeros((ELEM, ELEM), F32) for _ in range(FACES)]
    for g in range(FACES):
        column = key_ref[:, g : g + 1]
        for f in range(FACES):
            rank[f] = rank[f] + jnp.where(column < keys[f : f + 1, :], 1.0, 0.0)
    rows = iota((ROWS, ELEM), 0)
    slots = iota((FACES * ELEM, ELEM), 0)
    hi, mid, lo = thirds(trace_ref[...])
    stacked = jnp.concatenate([hi, mid, lo], axis=0)
    for f in range(FACES):
        own = cat[f : f + 1, :]
        pos = jnp.sum(rank[f], axis=0, keepdims=True).astype(I32)
        pos = pos + jnp.where(own > grp, GROUP_FACES, 0)
        pos = jnp.where(own == LOCAL, -1, pos)
        pos_ref[f : f + 1, :] = pos
        take_ref[:, f * ELEM : (f + 1) * ELEM] = onehot(rows == pos)
        inside = jnp.where(own == LOCAL, partner[f : f + 1, :], -1)
        got = dot_nn(stacked, onehot(slots == inside))
        near_ref[:, f * ELEM : (f + 1) * ELEM] = got[:128] + got[128:256] + got[256:]
    pos_ref[6:8, :] = jnp.zeros((2, ELEM), I32)


def section_kernel(
    grp_ref, pair0_ref, pair1_ref, base_ref, speed_ref, near_ref, take_ref, trace_ref, pick_ref, metric_ref, weight_ref,
    send_ref, send0_ref, send1_ref, sec_ref, donor_ref, mean_ref, outer_ref,
):
    got = jnp.concatenate([grp_ref[...], pair0_ref[...], pair1_ref[...]], axis=0).T
    hi, mid, lo = thirds(got)
    far = dot_nn(jnp.concatenate([hi, mid, lo], axis=0), take_ref[...])
    outer_ref[...] = near_ref[...] + far[:128] + far[128:256] + far[256:]
    half = (0.5 * LIFT_GAIN * SECTION_STEP) * metric_ref[...]
    sec_ref[...] = base_ref[...]
    for f in range(FACES):
        a = f // 2
        sign = 1.0 if f % 2 else -1.0
        inner = face_values(trace_ref, f)
        outer = face_values(outer_ref, f)
        inv, vel, pressure = primitives(outer)
        lam = half * jnp.maximum(speed_ref[f], speed(inv, vel, pressure, a))
        for v, row in enumerate(flux(outer, vel, pressure, a)):
            add_face(sec_ref, f, v, lam * (outer[v] - inner[v]) - (sign * half) * row)
    weight = weight_ref[...]
    for v in range(VARS):
        q = sec_ref[v]
        mean = jnp.sum(weight * q, axis=0, keepdims=True)
        dev = q - mean
        beta = 1e-06 + jnp.sum(weight * dev * dev, axis=0, keepdims=True)
        omega = 0.1 / (beta * beta)
        donor_ref[128 * v : 128 * v + NODES, :] = omega * dev
        donor_ref[128 * v + NODES : 128 * v + NODES + 1, :] = omega
        donor_ref[128 * v + NODES + 1 : 128 * v + 128, :] = jnp.zeros((2, ELEM), F32)
        mean_ref[v : v + 1, :] = mean
    sent = select_nt(pick_ref[...], donor_ref[...])
    send_ref[...] = sent[:GROUP_ROWS]
    send0_ref[...] = sent[PAIR0:PAIR1]
    send1_ref[...] = sent[PAIR1:]


def inside_kernel(
    elem_ref, troubled_ref, owner_ref, pos_ref, donor_ref,
    sum_ref, far_ref, move_ref, mask_ref,
):
    _, grp, left, right, odd = places()
    own = lax.axis_index("wide") * GROUP + grp
    elem = elem_ref[...]
    cells = jnp.where(troubled_ref[...] == iota((ELEM, 48), 0), 1.0, 0.0).astype(BF16)
    mask = dot_nt(jnp.ones((8, 48), BF16), cells)[0:1, :]
    mask_ref[0:1, :] = mask
    local = jnp.where(lax.shift_right_logical(elem, 7) == own, elem & (ELEM - 1), -1)
    rows = iota((ROWS, ELEM), 0)
    elems = iota((ELEM, ELEM), 0)
    near = jnp.zeros((ELEM, ELEM), F32)
    far = jnp.zeros((ROWS, ELEM), F32)
    for f in range(FACES):
        near = near + jnp.where(elems == local[f : f + 1, :], 1.0, 0.0)
        far = far + jnp.where(rows == pos_ref[f : f + 1, :], 1.0, 0.0)
    far_ref[...] = far.astype(BF16)
    near = near.astype(BF16)
    hi, mid, lo = thirds(donor_ref[...])
    sum_ref[...] = dot_nn(hi, near) + dot_nn(mid, near) + dot_nn(lo, near)
    owner = owner_ref[...]
    mask_ref[1:2, :] = jnp.where(owner == own, 1.0, 0.0)
    out0 = jnp.where(odd == 1, left, right)
    out1 = jnp.where(odd == 1, right, left)
    go0 = jnp.where(owner == out0, 1.0, 0.0)
    go1 = jnp.where(owner == out1, 1.0, 0.0)
    go = jnp.concatenate([go0, go1, jnp.zeros((6, ELEM), F32)], axis=0)
    order = dot_nn(go.astype(BF16), strict_upper())
    place = jnp.where(go0 > 0.5, order[0:1, :], jnp.where(go1 > 0.5, MOVE_CAP + order[1:2, :], -1.0))
    move_ref[...] = onehot(iota((2 * MOVE_CAP, ELEM), 0) == place.astype(I32))


def limit_kernel(
    grp_ref, pair0_ref, pair1_ref, sum_ref, far_ref, move_ref, mask_ref, donor_ref, mean_ref, sec_ref,
    limited_ref, go0_ref, go1_ref, flat_ref,
):
    got = jnp.concatenate([grp_ref[...], pair0_ref[...], pair1_ref[...]], axis=0)
    hi, mid, lo = thirds(got)
    far = far_ref[...]
    turned = far.astype(F32).T.astype(BF16)
    add = dot_nn(turned, hi) + dot_nn(turned, mid) + dot_nn(turned, lo)
    total = sum_ref[...] + add.T
    troubled = mask_ref[0:1, :] > 0.5
    for v in range(VARS):
        block = total[128 * v : 128 * v + 128]
        weights = block[NODES : NODES + 1]
        own = 4.0 * donor_ref[128 * v + NODES : 128 * v + NODES + 1, :]
        q = sec_ref[v]
        inv = 1.0 / (own + weights)
        value = (own * inv) * q + inv * block[:NODES] + (weights * inv) * mean_ref[v : v + 1, :]
        value = jnp.where(troubled, value, q)
        limited_ref[v] = value
        flat_ref[128 * v : 128 * v + NODES, :] = value
        flat_ref[128 * v + NODES : 128 * v + 128, :] = jnp.zeros((3, ELEM), F32)
    moved = select_nt(move_ref[...], flat_ref[...])
    go0_ref[...] = moved[:MOVE_CAP]
    go1_ref[...] = moved[MOVE_CAP:]


def keep_kernel(limited_ref, mask_ref, out_ref):
    stays = mask_ref[1:2, :] > 0.5
    for v in range(VARS):
        out_ref[v] = jnp.where(stays, limited_ref[v], 0.0)


def arrive_kernel(in0_ref, in1_ref, kept_ref, out_ref):
    odd = lax.rem(lax.axis_index("wide"), 2) == 1
    from_left = jnp.where(odd, in0_ref[...], in1_ref[...])
    from_right = jnp.where(odd, in1_ref[...], in0_ref[...])
    both = jnp.concatenate([from_left, from_right, jnp.zeros((64, VARS * 128), F32)], axis=0).T
    for v in range(VARS):
        out_ref[v] = both[128 * v : 128 * v + NODES]


VMEM = pl.BlockSpec(memory_space=pltpu.VMEM)


def call(kernel, shapes, scratch, *args):
    return pl.pallas_call(
        kernel,
        out_shape=[jax.ShapeDtypeStruct(shape, dtype) for shape, dtype in shapes],
        in_specs=[VMEM] * len(args),
        out_specs=[VMEM] * len(shapes),
        scratch_shapes=[pltpu.VMEM(shape, dtype) for shape, dtype in scratch],
        interpret=INTERPRET,
    )(*args)


def exchange(blocks, pair0, pair1):
    size = lax.axis_size("wide")
    first = [(i, i ^ 1) for i in range(size)]
    second = [(i, (i + 1) % size if i % 2 else (i - 1) % size) for i in range(size)]
    lanes = blocks.shape[1]
    got = lax.all_to_all(blocks.reshape(GROUP, GROUP_FACES, lanes), "grp", 0, 0)
    return (
        got.reshape(GROUP_ROWS, lanes),
        lax.ppermute(pair0, "wide", first),
        lax.ppermute(pair1, "wide", second),
    )


def swap(pair0, pair1):
    size = lax.axis_size("wide")
    first = [(i, i ^ 1) for i in range(size)]
    second = [(i, (i + 1) % size if i % 2 else (i - 1) % size) for i in range(size)]
    return lax.ppermute(pair0, "wide", first), lax.ppermute(pair1, "wide", second)


def shards(state, metric, nbr_elem, nbr_face, troubled, new_owner):
    diffs, weights = gll_tables()
    diff = np.zeros((128, 384), np.float32)
    for a in range(3):
        diff[:NODES, 128 * a : 128 * a + NODES] = diffs[a]
    diff = jnp.asarray(diff)
    weight = jnp.asarray(np.repeat(weights[:, None], ELEM, axis=1), F32)
    metric = metric.reshape(1, ELEM)
    troubled = troubled.reshape(1, 48)
    new_owner = new_owner.reshape(1, ELEM)
    cols = VARS * 128
    wide_lanes = FACES * ELEM

    blocks, pair0, pair1, trace, pick = call(
        pack_kernel,
        [((GROUP_ROWS, 128), F32), ((32, 128), F32), ((32, 128), F32), ((128, wide_lanes), F32), ((ROWS, ELEM), BF16)],
        [((ROWS, wide_lanes), BF16)],
        nbr_elem, state,
    )
    got, got0, got1 = exchange(blocks, pair0, pair1)
    base, speeds, near, take, pos = call(
        local_kernel,
        [((VARS, NODES, ELEM), F32), ((FACES, 25, ELEM), F32), ((128, wide_lanes), F32), ((ROWS, wide_lanes), BF16), ((8, ELEM), I32)],
        [((384, cols), F32), ((ELEM, 8), F32)],
        nbr_elem, nbr_face, state, metric, trace, diff,
    )
    blocks, pair0, pair1, sec, donor, mean = call(
        section_kernel,
        [((GROUP_ROWS, cols), F32), ((32, cols), F32), ((32, cols), F32), ((VARS, NODES, ELEM), F32), ((cols, ELEM), F32), ((8, ELEM), F32)],
        [((128, wide_lanes), F32)],
        got, got0, got1, base, speeds, near, take, trace, pick, metric, weight,
    )
    got, got0, got1 = exchange(blocks, pair0, pair1)
    total, far, move, mask = call(
        inside_kernel,
        [((cols, ELEM), F32), ((ROWS, ELEM), BF16), ((2 * MOVE_CAP, ELEM), BF16), ((8, ELEM), F32)],
        [],
        nbr_elem, troubled, new_owner, pos, donor,
    )
    limited, go0, go1 = call(
        limit_kernel,
        [((VARS, NODES, ELEM), F32), ((MOVE_CAP, cols), F32), ((MOVE_CAP, cols), F32)],
        [((cols, ELEM), F32)],
        got, got0, got1, total, far, move, mask, donor, mean, sec,
    )
    in0, in1 = swap(go0, go1)
    out_shape = jax.ShapeDtypeStruct((VARS, NODES, ELEM + 2 * MOVE_CAP), F32)
    whole = lambda shape: pl.BlockSpec(shape, lambda i: (0,) * len(shape))
    kept = pl.pallas_call(
        keep_kernel,
        out_shape=out_shape,
        grid=(1,),
        in_specs=[whole((VARS, NODES, ELEM)), whole((8, ELEM))],
        out_specs=pl.BlockSpec((VARS, NODES, ELEM), lambda i: (0, 0, 0)),
        interpret=INTERPRET,
    )(limited, mask)
    return pl.pallas_call(
        arrive_kernel,
        out_shape=out_shape,
        grid=(1,),
        in_specs=[whole((MOVE_CAP, cols)), whole((MOVE_CAP, cols)), pl.BlockSpec(memory_space=pl.ANY)],
        out_specs=pl.BlockSpec((VARS, NODES, ELEM), lambda i: (0, 0, 1)),
        input_output_aliases={2: 0},
        interpret=INTERPRET,
    )(in0, in1, kept)


def solution(mesh):
    placed = (
        P(None, None, ("wide", "grp")),
        P(("wide", "grp")),
        P(None, ("wide", "grp")),
        P(None, ("wide", "grp")),
        P(("wide", "grp")),
        P(("wide", "grp")),
    )
    return jax.shard_map(
        shards,
        mesh=mesh,
        in_specs=placed,
        out_specs=P(None, None, ("wide", "grp")),
        check_vma=False,
    )
```

```python
import functools
import math

import jax
import jax.numpy as jnp
import numpy as np
from jax import lax
from jax.experimental import pallas as pl
from jax.experimental.pallas import tpu as pltpu
from jax.sharding import PartitionSpec as P

GROUP_FACES = 16
WIDE_FACES = 32
MOVE_CAP = 32
SECTION_STEP = 0.01
LIFT_GAIN = 10.0

ELEM = 128
VARS = 5
NODES = 125
FACES = 6
GROUP = 8
GROUP_ROWS = GROUP * GROUP_FACES
PAIR0 = GROUP_ROWS
PAIR1 = GROUP_ROWS + WIDE_FACES
ROWS = GROUP_ROWS + 2 * WIDE_FACES
LOCAL = 10

F32 = jnp.float32
BF16 = jnp.bfloat16
I32 = jnp.int32
INTERPRET = False


def gll_tables():
    root = math.sqrt(3.0 / 7.0)
    points = np.array([-1.0, -root, 0.0, root, 1.0])
    weights = np.array([0.1, 49.0 / 90.0, 32.0 / 45.0, 49.0 / 90.0, 0.1])
    bary = np.array(
        [1.0 / np.prod([points[j] - points[k] for k in range(5) if k != j]) for j in range(5)]
    )
    deriv = np.zeros((5, 5))
    for i in range(5):
        for j in range(5):
            if i != j:
                deriv[i, j] = bary[j] / bary[i] / (points[i] - points[j])
        deriv[i, i] = -np.sum(deriv[i])
    ident = np.eye(5)
    diffs = [
        np.kron(np.kron(deriv, ident), ident),
        np.kron(np.kron(ident, deriv), ident),
        np.kron(np.kron(ident, ident), deriv),
    ]
    cell_weights = np.kron(np.kron(weights, weights), weights) / 8.0
    return diffs, cell_weights


def face_rows(face):
    if face < 2:
        return [(100 * face, 25, 1, 0)]
    if face < 4:
        return [(25 * a + 20 * (face - 2), 5, 1, 5 * a) for a in range(5)]
    return [(4 * (face - 4), 25, 5, 0)]


def rows_at(first, count, stride):
    return pl.ds(first, count) if stride == 1 else pl.ds(first, count, stride=stride)


def thirds(x):
    hi = x.astype(BF16)
    rest = x - hi.astype(F32)
    mid = rest.astype(BF16)
    lo = (rest - mid.astype(F32)).astype(BF16)
    return hi, mid, lo


def dot_nn(a, b):
    return lax.dot_general(a, b, (((1,), (0,)), ((), ())), preferred_element_type=F32)


def dot_nt(a, b):
    return lax.dot_general(a, b, (((1,), (1,)), ((), ())), preferred_element_type=F32)


def select_nt(onehot, values):
    hi, mid, lo = thirds(values)
    return dot_nt(onehot, hi) + dot_nt(onehot, mid) + dot_nt(onehot, lo)


def iota(shape, dim):
    return lax.broadcasted_iota(I32, shape, dim)


def onehot(mask):
    return jnp.where(mask, 1.0, 0.0).astype(BF16)


def places():
    wide = lax.axis_index("wide")
    grp = lax.axis_index("grp")
    size = lax.axis_size("wide")
    left = lax.rem(wide + size - 1, size) * GROUP + grp
    right = lax.rem(wide + 1, size) * GROUP + grp
    odd = lax.rem(wide, 2)
    return wide, grp, left, right, odd


def categories(nbr_elem):
    wide, grp, left, _, odd = places()
    owner = lax.shift_right_logical(nbr_elem, 7)
    beside = jnp.where(owner == left, 9 - odd, 8 + odd)
    cat = jnp.where(lax.shift_right_logical(owner, 3) == wide, owner & 7, beside)
    return jnp.where(owner == wide * GROUP + grp, LOCAL, cat)


def strict_upper():
    return onehot(iota((ELEM, ELEM), 0) < iota((ELEM, ELEM), 1))


def pack_kernel(elem_ref, state_ref, grp_ref, pair0_ref, pair1_ref, trace_ref, pick_ref, s_ref):
    cat = categories(elem_ref[...])
    kinds = iota((16, ELEM), 0)
    hot = [jnp.where(cat[f : f + 1, :] == kinds, 1.0, 0.0) for f in range(FACES)]
    upper = jnp.concatenate([strict_upper(), jnp.ones((ELEM, ELEM), BF16)], axis=1)
    counts = dot_nn(jnp.concatenate(hot, axis=0).astype(BF16), upper)
    base = jnp.where(kinds < 9, 16 * kinds, PAIR1).astype(F32)
    pick = jnp.zeros((ROWS, ELEM), F32)
    rows = iota((ROWS, ELEM), 0)
    for f in range(FACES):
        part = counts[16 * f : 16 * f + 16]
        pos = jnp.sum(hot[f] * (part[:, :ELEM] + base), axis=0, keepdims=True)
        base = base + part[:, ELEM:]
        pos = jnp.where(cat[f : f + 1, :] == LOCAL, -1, pos.astype(I32))
        chosen = jnp.where(rows == pos, 1.0, 0.0)
        pick = pick + chosen
        s_ref[:, f * ELEM : (f + 1) * ELEM] = chosen.astype(BF16)
    pick_ref[...] = pick.astype(BF16)
    for f in range(FACES):
        for v in range(VARS):
            for first, count, stride, place in face_rows(f):
                trace_ref[25 * v + place : 25 * v + place + count, f * ELEM : (f + 1) * ELEM] = state_ref[
                    v, rows_at(first, count, stride), :
                ]
    trace_ref[125:128, :] = jnp.zeros((3, FACES * ELEM), F32)
    sent = select_nt(s_ref[...], trace_ref[...])
    grp_ref[...] = sent[:GROUP_ROWS]
    pair0_ref[...] = sent[PAIR0:PAIR1]
    pair1_ref[...] = sent[PAIR1:]


def primitives(u):
    inv = 1.0 / u[0]
    vel = [u[1] * inv, u[2] * inv, u[3] * inv]
    kinetic = u[1] * vel[0] + u[2] * vel[1] + u[3] * vel[2]
    pressure = 0.4 * (u[4] - 0.5 * kinetic)
    return inv, vel, pressure


def flux(u, vel, pressure, a):
    w = vel[a]
    rows = [u[1 + a], u[1] * w, u[2] * w, u[3] * w, (u[4] + pressure) * w]
    rows[1 + a] = rows[1 + a] + pressure
    return rows


def speed(inv, vel, pressure, a):
    return jnp.abs(vel[a]) + jnp.sqrt(1.4 * pressure * inv)


def face_values(ref, f):
    return [ref[25 * v : 25 * v + 25, f * ELEM : (f + 1) * ELEM] for v in range(VARS)]


def add_face(ref, f, v, value):
    for first, count, stride, place in face_rows(f):
        at = rows_at(first, count, stride)
        ref[v, at, :] = ref[v, at, :] + value[place : place + count]


def local_kernel(
    elem_ref, face_ref, state_ref, metric_ref, trace_ref, diff_ref,
    base_ref, speed_ref, near_ref, take_ref, pos_ref, f_ref, key_ref,
):
    metric = metric_ref[...]
    u = [state_ref[v] for v in range(VARS)]
    inv, vel, pressure = primitives(u)
    for a in range(3):
        for v, row in enumerate(flux(u, vel, pressure, a)):
            f_ref[128 * a : 128 * a + NODES, v * ELEM : (v + 1) * ELEM] = row
        f_ref[128 * a + NODES : 128 * a + 128, :] = jnp.zeros((3, VARS * ELEM), F32)
    volume = jnp.dot(diff_ref[...], f_ref[...], precision=lax.Precision.HIGHEST, preferred_element_type=F32)
    for v in range(VARS):
        base_ref[v] = u[v] - (SECTION_STEP * metric) * volume[:NODES, v * ELEM : (v + 1) * ELEM]
    half = (0.5 * LIFT_GAIN * SECTION_STEP) * metric
    for f in range(FACES):
        a = f // 2
        scale = half if f % 2 else -half
        inner = face_values(trace_ref, f)
        inv, vel, pressure = primitives(inner)
        speed_ref[f] = speed(inv, vel, pressure, a)
        for v, row in enumerate(flux(inner, vel, pressure, a)):
            add_face(base_ref, f, v, scale * row)
    cat = categories(elem_ref[...])
    partner = face_ref[...] * ELEM + (elem_ref[...] & (ELEM - 1))
    _, grp, _, _, _ = places()
    key = jnp.concatenate([cat * (FACES * ELEM) + partner, jnp.zeros((2, ELEM), I32)], axis=0)
    key_ref[...] = key.astype(F32).T
    keys = key.astype(F32)
    rank = [jnp.zeros((ELEM, ELEM), F32) for _ in range(FACES)]
    for g in range(FACES):
        column = key_ref[:, g : g + 1]
        for f in range(FACES):
            rank[f] = rank[f] + jnp.where(column < keys[f : f + 1, :], 1.0, 0.0)
    rows = iota((ROWS, ELEM), 0)
    slots = iota((FACES * ELEM, ELEM), 0)
    hi, mid, lo = thirds(trace_ref[...])
    stacked = jnp.concatenate([hi, mid, lo], axis=0)
    for f in range(FACES):
        own = cat[f : f + 1, :]
        pos = jnp.sum(rank[f], axis=0, keepdims=True).astype(I32)
        pos = pos + jnp.where(own > grp, GROUP_FACES, 0)
        pos = jnp.where(own == LOCAL, -1, pos)
        pos_ref[f : f + 1, :] = pos
        take_ref[:, f * ELEM : (f + 1) * ELEM] = onehot(rows == pos)
        inside = jnp.where(own == LOCAL, partner[f : f + 1, :], -1)
        got = dot_nn(stacked, onehot(slots == inside))
        near_ref[:, f * ELEM : (f + 1) * ELEM] = got[:128] + got[128:256] + got[256:]
    pos_ref[6:8, :] = jnp.zeros((2, ELEM), I32)


def section_kernel(
    grp_ref, pair0_ref, pair1_ref, base_ref, speed_ref, near_ref, take_ref, trace_ref, pick_ref, metric_ref, weight_ref,
    send_ref, send0_ref, send1_ref, sec_ref, donor_ref, mean_ref, outer_ref,
):
    got = jnp.concatenate([grp_ref[...], pair0_ref[...], pair1_ref[...]], axis=0).T
    hi, mid, lo = thirds(got)
    far = dot_nn(jnp.concatenate([hi, mid, lo], axis=0), take_ref[...])
    outer_ref[...] = near_ref[...] + far[:128] + far[128:256] + far[256:]
    half = (0.5 * LIFT_GAIN * SECTION_STEP) * metric_ref[...]
    sec_ref[...] = base_ref[...]
    for f in range(FACES):
        a = f // 2
        sign = 1.0 if f % 2 else -1.0
        inner = face_values(trace_ref, f)
        outer = face_values(outer_ref, f)
        inv, vel, pressure = primitives(outer)
        lam = half * jnp.maximum(speed_ref[f], speed(inv, vel, pressure, a))
        for v, row in enumerate(flux(outer, vel, pressure, a)):
            add_face(sec_ref, f, v, lam * (outer[v] - inner[v]) - (sign * half) * row)
    weight = weight_ref[...]
    for v in range(VARS):
        q = sec_ref[v]
        mean = jnp.sum(weight * q, axis=0, keepdims=True)
        dev = q - mean
        beta = 1e-06 + jnp.sum(weight * dev * dev, axis=0, keepdims=True)
        omega = 0.1 / (beta * beta)
        donor_ref[128 * v : 128 * v + NODES, :] = omega * dev
        donor_ref[128 * v + NODES : 128 * v + NODES + 1, :] = omega
        donor_ref[128 * v + NODES + 1 : 128 * v + 128, :] = jnp.zeros((2, ELEM), F32)
        mean_ref[v : v + 1, :] = mean
    sent = select_nt(pick_ref[...], donor_ref[...])
    send_ref[...] = sent[:GROUP_ROWS]
    send0_ref[...] = sent[PAIR0:PAIR1]
    send1_ref[...] = sent[PAIR1:]


def inside_kernel(
    elem_ref, troubled_ref, owner_ref, pos_ref, donor_ref, mean_ref, sec_ref,
    sum_ref, still_ref, far_ref, move_ref, cell_ref, wide_ref,
):
    _, grp, left, right, odd = places()
    own = lax.axis_index("wide") * GROUP + grp
    elem = elem_ref[...]
    troubled = jnp.sum(
        jnp.where(troubled_ref[...] == iota((ELEM, 48), 0), 1.0, 0.0), axis=1, keepdims=True
    )
    local = jnp.where(lax.shift_right_logical(elem, 7) == own, elem & (ELEM - 1), -1)
    rows = iota((ROWS, ELEM), 0)
    elems = iota((ELEM, ELEM), 0)
    near = jnp.where(elems == iota((ELEM, ELEM), 1), 4.0, 0.0)
    far = jnp.zeros((ROWS, ELEM), F32)
    for f in range(FACES):
        near = near + jnp.where(elems == local[f : f + 1, :], 1.0, 0.0)
        far = far + jnp.where(rows == pos_ref[f : f + 1, :], 1.0, 0.0)
    far_ref[...] = jnp.concatenate([far, jnp.zeros((64, ELEM), F32)], axis=0).T[:, :ROWS].astype(BF16)
    sum_ref[...] = select_nt(near.T.astype(BF16), donor_ref[...])
    for v in range(VARS):
        wide_ref[0:NODES, :] = sec_ref[v]
        wide_ref[NODES:128, :] = jnp.zeros((3, ELEM), F32)
        value = wide_ref[...].T
        mean = jnp.broadcast_to(mean_ref[v : v + 1, :], (ELEM, ELEM)).T
        still_ref[:, 128 * v : 128 * v + 128] = jnp.where(troubled > 0.5, mean, value)
    owner = owner_ref[...]
    out0 = jnp.where(odd == 1, left, right)
    out1 = jnp.where(odd == 1, right, left)
    stays = jnp.where(owner == own, 1.0, 0.0)
    cell_ref[:, 0:128] = jnp.broadcast_to(troubled, (ELEM, ELEM))
    cell_ref[:, 128:256] = jnp.broadcast_to(stays, (ELEM, ELEM)).T
    go0 = jnp.where(owner == out0, 1.0, 0.0)
    go1 = jnp.where(owner == out1, 1.0, 0.0)
    go = jnp.concatenate([go0, go1, jnp.zeros((6, ELEM), F32)], axis=0)
    order = dot_nn(go.astype(BF16), strict_upper())
    place = jnp.where(go0 > 0.5, order[0:1, :], jnp.where(go1 > 0.5, MOVE_CAP + order[1:2, :], -1.0))
    move_ref[...] = onehot(iota((2 * MOVE_CAP, ELEM), 0) == place.astype(I32))


def limit_kernel(
    grp_ref, pair0_ref, pair1_ref, sum_ref, still_ref, far_ref, move_ref, cell_ref,
    limited_ref, go0_ref, go1_ref,
):
    got = jnp.concatenate([grp_ref[...], pair0_ref[...], pair1_ref[...]], axis=0)
    hi, mid, lo = thirds(got)
    far = far_ref[...]
    total = sum_ref[...] + (dot_nn(far, hi) + dot_nn(far, mid) + dot_nn(far, lo))
    troubled = cell_ref[:, 0:1] > 0.5
    for v in range(VARS):
        cols = slice(128 * v, 128 * v + 128)
        scale = jnp.where(troubled, 1.0 / total[:, 128 * v + NODES : 128 * v + NODES + 1], 0.0)
        limited_ref[:, cols] = still_ref[:, cols] + scale * total[:, cols]
    hi, mid, lo = thirds(limited_ref[...])
    move = move_ref[...]
    moved = dot_nn(move, hi) + dot_nn(move, mid) + dot_nn(move, lo)
    go0_ref[...] = moved[:MOVE_CAP]
    go1_ref[...] = moved[MOVE_CAP:]


def keep_kernel(limited_ref, cell_ref, out_ref):
    stays = cell_ref[:, 128:256] > 0.5
    for v in range(VARS):
        out_ref[v] = jnp.where(stays, limited_ref[:, 128 * v : 128 * v + 128], 0.0)[:, :NODES]


def arrive_kernel(in0_ref, in1_ref, kept_ref, out_ref):
    odd = lax.rem(lax.axis_index("wide"), 2) == 1
    from_left = jnp.where(odd, in0_ref[...], in1_ref[...])
    from_right = jnp.where(odd, in1_ref[...], in0_ref[...])
    for v in range(VARS):
        out_ref[v, 0:MOVE_CAP, :] = from_left[:, 128 * v : 128 * v + NODES]
        out_ref[v, MOVE_CAP:, :] = from_right[:, 128 * v : 128 * v + NODES]


VMEM = pl.BlockSpec(memory_space=pltpu.VMEM)
PARAMS = pltpu.CompilerParams(vmem_limit_bytes=16 * 1024 * 1024)


def call(kernel, shapes, scratch, *args):
    args = [pltpu.with_memory_space_constraint(arg, pltpu.VMEM) for arg in args]
    return pl.pallas_call(
        kernel,
        out_shape=[pltpu.VMEM(shape, dtype) for shape, dtype in shapes],
        in_specs=[VMEM] * len(args),
        out_specs=[VMEM] * len(shapes),
        scratch_shapes=[pltpu.VMEM(shape, dtype) for shape, dtype in scratch],
        compiler_params=PARAMS,
        interpret=INTERPRET,
    )(*args)


def exchange(blocks, pair0, pair1):
    size = lax.axis_size("wide")
    first = [(i, i ^ 1) for i in range(size)]
    second = [(i, (i + 1) % size if i % 2 else (i - 1) % size) for i in range(size)]
    lanes = blocks.shape[1]
    got = lax.all_to_all(blocks.reshape(GROUP, GROUP_FACES, lanes), "grp", 0, 0)
    return (
        got.reshape(GROUP_ROWS, lanes),
        lax.ppermute(pair0, "wide", first),
        lax.ppermute(pair1, "wide", second),
    )


def swap(pair0, pair1):
    size = lax.axis_size("wide")
    first = [(i, i ^ 1) for i in range(size)]
    second = [(i, (i + 1) % size if i % 2 else (i - 1) % size) for i in range(size)]
    return lax.ppermute(pair0, "wide", first), lax.ppermute(pair1, "wide", second)


def shards(state, metric, nbr_elem, nbr_face, troubled, new_owner):
    diffs, weights = gll_tables()
    diff = np.zeros((128, 384), np.float32)
    for a in range(3):
        diff[:NODES, 128 * a : 128 * a + NODES] = diffs[a]
    diff = jnp.asarray(diff)
    weight = jnp.asarray(np.repeat(weights[:, None], ELEM, axis=1), F32)
    metric = metric.reshape(1, ELEM)
    troubled = troubled.reshape(1, 48)
    new_owner = new_owner.reshape(1, ELEM)
    cols = VARS * 128
    wide_lanes = FACES * ELEM

    blocks, pair0, pair1, trace, pick = call(
        pack_kernel,
        [((GROUP_ROWS, 128), F32), ((32, 128), F32), ((32, 128), F32), ((128, wide_lanes), F32), ((ROWS, ELEM), BF16)],
        [((ROWS, wide_lanes), BF16)],
        nbr_elem, state,
    )
    got, got0, got1 = exchange(blocks, pair0, pair1)
    base, speeds, near, take, pos = call(
        local_kernel,
        [((VARS, NODES, ELEM), F32), ((FACES, 25, ELEM), F32), ((128, wide_lanes), F32), ((ROWS, wide_lanes), BF16), ((8, ELEM), I32)],
        [((384, cols), F32), ((ELEM, 8), F32)],
        nbr_elem, nbr_face, state, metric, trace, diff,
    )
    blocks, pair0, pair1, sec, donor, mean = call(
        section_kernel,
        [((GROUP_ROWS, cols), F32), ((32, cols), F32), ((32, cols), F32), ((VARS, NODES, ELEM), F32), ((cols, ELEM), F32), ((8, ELEM), F32)],
        [((128, wide_lanes), F32)],
        got, got0, got1, base, speeds, near, take, trace, pick, metric, weight,
    )
    got, got0, got1 = exchange(blocks, pair0, pair1)
    total, still, far, move, cell = call(
        inside_kernel,
        [((ELEM, cols), F32), ((ELEM, cols), F32), ((ELEM, ROWS), BF16), ((2 * MOVE_CAP, ELEM), BF16), ((ELEM, 256), F32)],
        [((128, ELEM), F32)],
        nbr_elem, troubled, new_owner, pos, donor, mean, sec,
    )
    limited, go0, go1 = call(
        limit_kernel,
        [((ELEM, cols), F32), ((MOVE_CAP, cols), F32), ((MOVE_CAP, cols), F32)],
        [],
        got, got0, got1, total, still, far, move, cell,
    )
    in0, in1 = swap(go0, go1)
    out_shape = jax.ShapeDtypeStruct((VARS, ELEM + 2 * MOVE_CAP, NODES), F32)
    vmem = lambda x: pltpu.with_memory_space_constraint(x, pltpu.VMEM)
    kept = pl.pallas_call(
        keep_kernel,
        out_shape=out_shape,
        grid=(1,),
        in_specs=[VMEM, VMEM],
        out_specs=pl.BlockSpec((VARS, ELEM, NODES), lambda i: (0, 0, 0)),
        compiler_params=PARAMS,
        interpret=INTERPRET,
    )(vmem(limited), vmem(cell))
    moved = pl.pallas_call(
        arrive_kernel,
        out_shape=out_shape,
        grid=(1,),
        in_specs=[VMEM, VMEM, pl.BlockSpec(memory_space=pl.ANY)],
        out_specs=pl.BlockSpec((VARS, 2 * MOVE_CAP, NODES), lambda i: (0, 2, 0)),
        input_output_aliases={2: 0},
        compiler_params=PARAMS,
        interpret=INTERPRET,
    )(vmem(in0), vmem(in1), kept)
    return jnp.transpose(moved, (0, 2, 1))


def solution(mesh):
    placed = (
        P(None, None, ("wide", "grp")),
        P(("wide", "grp")),
        P(None, ("wide", "grp")),
        P(None, ("wide", "grp")),
        P(("wide", "grp")),
        P(("wide", "grp")),
    )
    return jax.shard_map(
        shards,
        mesh=mesh,
        in_specs=placed,
        out_specs=P(None, None, ("wide", "grp")),
        check_vma=False,
    )
```

```python
import math

import jax
import jax.numpy as jnp
import numpy as np
from jax import lax
from jax.experimental import pallas as pl
from jax.experimental.pallas import tpu as pltpu
from jax.sharding import PartitionSpec as P


GROUP_FACES = 16
WIDE_FACES = 32
MOVE_CAP = 32
SECTION_STEP = 0.01
LIFT_GAIN = 10.0

ELEM = 128
VARS = 5
NODES = 125
FACES = 6
GROUP = 8
GROUP_ROWS = GROUP * GROUP_FACES
PAIR0 = GROUP_ROWS
PAIR1 = GROUP_ROWS + WIDE_FACES
ROWS = GROUP_ROWS + 2 * WIDE_FACES
LOCAL = 10

F32 = jnp.float32
BF16 = jnp.bfloat16
I32 = jnp.int32
INTERPRET = False


def gll_tables():
    root = math.sqrt(3.0 / 7.0)
    points = np.array([-1.0, -root, 0.0, root, 1.0])
    weights = np.array([0.1, 49.0 / 90.0, 32.0 / 45.0, 49.0 / 90.0, 0.1])
    bary = np.array(
        [1.0 / np.prod([points[j] - points[k] for k in range(5) if k != j]) for j in range(5)]
    )
    deriv = np.zeros((5, 5))
    for i in range(5):
        for j in range(5):
            if i != j:
                deriv[i, j] = bary[j] / bary[i] / (points[i] - points[j])
        deriv[i, i] = -np.sum(deriv[i])
    ident = np.eye(5)
    diffs = [
        np.kron(np.kron(deriv, ident), ident),
        np.kron(np.kron(ident, deriv), ident),
        np.kron(np.kron(ident, ident), deriv),
    ]
    cell_weights = np.kron(np.kron(weights, weights), weights) / 8.0
    return diffs, cell_weights


def face_rows(face):
    if face < 2:
        return [(100 * face, 25, 1, 0)]
    if face < 4:
        return [(25 * a + 20 * (face - 2), 5, 1, 5 * a) for a in range(5)]
    return [(4 * (face - 4), 25, 5, 0)]


def rows_at(first, count, stride):
    return pl.ds(first, count) if stride == 1 else pl.ds(first, count, stride=stride)


def thirds(x):
    hi = x.astype(BF16)
    rest = x - hi.astype(F32)
    mid = rest.astype(BF16)
    lo = (rest - mid.astype(F32)).astype(BF16)
    return hi, mid, lo


def dot_nn(a, b):
    return lax.dot_general(a, b, (((1,), (0,)), ((), ())), preferred_element_type=F32)


def dot_nt(a, b):
    return lax.dot_general(a, b, (((1,), (1,)), ((), ())), preferred_element_type=F32)


def select_nt(onehot, values):
    hi, mid, lo = thirds(values)
    return dot_nt(onehot, hi) + dot_nt(onehot, mid) + dot_nt(onehot, lo)


def iota(shape, dim):
    return lax.broadcasted_iota(I32, shape, dim)


def onehot(mask):
    return jnp.where(mask, 1.0, 0.0).astype(BF16)


def places():
    wide = lax.axis_index("wide")
    grp = lax.axis_index("grp")
    size = lax.axis_size("wide")
    left = lax.rem(wide + size - 1, size) * GROUP + grp
    right = lax.rem(wide + 1, size) * GROUP + grp
    odd = lax.rem(wide, 2)
    return wide, grp, left, right, odd


def categories(nbr_elem):
    wide, grp, left, _, odd = places()
    owner = lax.shift_right_logical(nbr_elem, 7)
    beside = jnp.where(owner == left, 9 - odd, 8 + odd)
    cat = jnp.where(lax.shift_right_logical(owner, 3) == wide, owner & 7, beside)
    return jnp.where(owner == wide * GROUP + grp, LOCAL, cat)


def strict_upper():
    return onehot(iota((ELEM, ELEM), 0) < iota((ELEM, ELEM), 1))


def pack_kernel(
    elem_hbm, state_hbm, face_hbm, metric_hbm, troubled_hbm, owner_hbm, diff_hbm, weight_hbm,
    grp_ref, pair0_ref, pair1_ref, trace_ref, pick_ref,
    elem_ref, state_ref, face_ref, metric_ref, troubled_ref, owner_ref, diff_ref, weight_ref,
    s_ref, sems,
):
    first = pltpu.make_async_copy(elem_hbm, elem_ref, sems.at[0])
    first.start()
    second = pltpu.make_async_copy(state_hbm, state_ref, sems.at[1])
    second.start()
    later = []
    for k, (source, target) in enumerate(
        (
            (face_hbm, face_ref),
            (metric_hbm, metric_ref),
            (troubled_hbm, troubled_ref),
            (owner_hbm, owner_ref),
            (diff_hbm, diff_ref),
            (weight_hbm, weight_ref),
        )
    ):
        copy = pltpu.make_async_copy(source, target, sems.at[2 + k])
        copy.start()
        later.append(copy)
    first.wait()
    cat = categories(elem_ref[...])
    kinds = iota((16, ELEM), 0)
    hot = [jnp.where(cat[f : f + 1, :] == kinds, 1.0, 0.0) for f in range(FACES)]
    upper = jnp.concatenate([strict_upper(), jnp.ones((ELEM, ELEM), BF16)], axis=1)
    counts = dot_nn(jnp.concatenate(hot, axis=0).astype(BF16), upper)
    base = jnp.where(kinds < 9, 16 * kinds, PAIR1).astype(F32)
    pick = jnp.zeros((ROWS, ELEM), F32)
    rows = iota((ROWS, ELEM), 0)
    for f in range(FACES):
        part = counts[16 * f : 16 * f + 16]
        pos = jnp.sum(hot[f] * (part[:, :ELEM] + base), axis=0, keepdims=True)
        base = base + part[:, ELEM:]
        pos = jnp.where(cat[f : f + 1, :] == LOCAL, -1, pos.astype(I32))
        chosen = jnp.where(rows == pos, 1.0, 0.0)
        pick = pick + chosen
        s_ref[:, f * ELEM : (f + 1) * ELEM] = chosen.astype(BF16)
    pick_ref[...] = pick.astype(BF16)
    second.wait()
    for f in range(FACES):
        for v in range(VARS):
            for first, count, stride, place in face_rows(f):
                trace_ref[25 * v + place : 25 * v + place + count, f * ELEM : (f + 1) * ELEM] = state_ref[
                    v, rows_at(first, count, stride), :
                ]
    trace_ref[125:128, :] = jnp.zeros((3, FACES * ELEM), F32)
    sent = select_nt(s_ref[...], trace_ref[...])
    grp_ref[...] = sent[:GROUP_ROWS]
    pair0_ref[...] = sent[PAIR0:PAIR1]
    pair1_ref[...] = sent[PAIR1:]
    for copy in later:
        copy.wait()


def primitives(u):
    inv = 1.0 / u[0]
    vel = [u[1] * inv, u[2] * inv, u[3] * inv]
    kinetic = u[1] * vel[0] + u[2] * vel[1] + u[3] * vel[2]
    pressure = 0.4 * (u[4] - 0.5 * kinetic)
    return inv, vel, pressure


def flux(u, vel, pressure, a):
    w = vel[a]
    rows = [u[1 + a], u[1] * w, u[2] * w, u[3] * w, (u[4] + pressure) * w]
    rows[1 + a] = rows[1 + a] + pressure
    return rows


def speed(inv, vel, pressure, a):
    return jnp.abs(vel[a]) + jnp.sqrt(1.4 * pressure * inv)


def face_values(ref, f):
    return [ref[25 * v : 25 * v + 25, f * ELEM : (f + 1) * ELEM] for v in range(VARS)]


def add_face(ref, f, v, value):
    for first, count, stride, place in face_rows(f):
        at = rows_at(first, count, stride)
        ref[v, at, :] = ref[v, at, :] + value[place : place + count]


def local_kernel(
    elem_ref, face_ref, state_ref, metric_ref, trace_ref, diff_ref,
    base_ref, speed_ref, near_ref, take_ref, pos_ref, f_ref, key_ref,
):
    metric = metric_ref[...]
    u = [state_ref[v] for v in range(VARS)]
    inv, vel, pressure = primitives(u)
    for a in range(3):
        for v, row in enumerate(flux(u, vel, pressure, a)):
            f_ref[128 * a : 128 * a + NODES, v * ELEM : (v + 1) * ELEM] = row
        f_ref[128 * a + NODES : 128 * a + 128, :] = jnp.zeros((3, VARS * ELEM), F32)
    volume = jnp.dot(diff_ref[...], f_ref[...], precision=lax.Precision.HIGHEST, preferred_element_type=F32)
    for v in range(VARS):
        base_ref[v] = u[v] - (SECTION_STEP * metric) * volume[:NODES, v * ELEM : (v + 1) * ELEM]
    half = (0.5 * LIFT_GAIN * SECTION_STEP) * metric
    for f in range(FACES):
        a = f // 2
        scale = half if f % 2 else -half
        inner = face_values(trace_ref, f)
        inv, vel, pressure = primitives(inner)
        speed_ref[f] = speed(inv, vel, pressure, a)
        for v, row in enumerate(flux(inner, vel, pressure, a)):
            add_face(base_ref, f, v, scale * row)
    cat = categories(elem_ref[...])
    partner = face_ref[...] * ELEM + (elem_ref[...] & (ELEM - 1))
    _, grp, _, _, _ = places()
    key = jnp.concatenate([cat * (FACES * ELEM) + partner, jnp.zeros((2, ELEM), I32)], axis=0)
    key_ref[...] = key.astype(F32).T
    keys = key.astype(F32)
    rank = [jnp.zeros((ELEM, ELEM), F32) for _ in range(FACES)]
    for g in range(FACES):
        column = key_ref[:, g : g + 1]
        for f in range(FACES):
            rank[f] = rank[f] + jnp.where(column < keys[f : f + 1, :], 1.0, 0.0)
    rows = iota((ROWS, ELEM), 0)
    slots = iota((FACES * ELEM, ELEM), 0)
    hi, mid, lo = thirds(trace_ref[...])
    stacked = jnp.concatenate([hi, mid, lo], axis=0)
    for f in range(FACES):
        own = cat[f : f + 1, :]
        pos = jnp.sum(rank[f], axis=0, keepdims=True).astype(I32)
        pos = pos + jnp.where(own > grp, GROUP_FACES, 0)
        pos = jnp.where(own == LOCAL, -1, pos)
        pos_ref[f : f + 1, :] = pos
        take_ref[:, f * ELEM : (f + 1) * ELEM] = onehot(rows == pos)
        inside = jnp.where(own == LOCAL, partner[f : f + 1, :], -1)
        got = dot_nn(stacked, onehot(slots == inside))
        near_ref[:, f * ELEM : (f + 1) * ELEM] = got[:128] + got[128:256] + got[256:]
    pos_ref[6:8, :] = jnp.zeros((2, ELEM), I32)


def section_kernel(
    grp_ref, pair0_ref, pair1_ref, base_ref, speed_ref, near_ref, take_ref, trace_ref, pick_ref, metric_ref, weight_ref,
    send_ref, send0_ref, send1_ref, sec_ref, donor_ref, mean_ref, outer_ref,
):
    got = jnp.concatenate([grp_ref[...], pair0_ref[...], pair1_ref[...]], axis=0).T
    hi, mid, lo = thirds(got)
    far = dot_nn(jnp.concatenate([hi, mid, lo], axis=0), take_ref[...])
    outer_ref[...] = near_ref[...] + far[:128] + far[128:256] + far[256:]
    half = (0.5 * LIFT_GAIN * SECTION_STEP) * metric_ref[...]
    sec_ref[...] = base_ref[...]
    for f in range(FACES):
        a = f // 2
        sign = 1.0 if f % 2 else -1.0
        inner = face_values(trace_ref, f)
        outer = face_values(outer_ref, f)
        inv, vel, pressure = primitives(outer)
        lam = half * jnp.maximum(speed_ref[f], speed(inv, vel, pressure, a))
        for v, row in enumerate(flux(outer, vel, pressure, a)):
            add_face(sec_ref, f, v, lam * (outer[v] - inner[v]) - (sign * half) * row)
    weight = weight_ref[...]
    for v in range(VARS):
        q = sec_ref[v]
        mean = jnp.sum(weight * q, axis=0, keepdims=True)
        dev = q - mean
        beta = 1e-06 + jnp.sum(weight * dev * dev, axis=0, keepdims=True)
        omega = 0.1 / (beta * beta)
        donor_ref[128 * v : 128 * v + NODES, :] = omega * dev
        donor_ref[128 * v + NODES : 128 * v + NODES + 1, :] = omega
        donor_ref[128 * v + NODES + 1 : 128 * v + 128, :] = jnp.zeros((2, ELEM), F32)
        mean_ref[v : v + 1, :] = mean
    sent = select_nt(pick_ref[...], donor_ref[...])
    send_ref[...] = sent[:GROUP_ROWS]
    send0_ref[...] = sent[PAIR0:PAIR1]
    send1_ref[...] = sent[PAIR1:]


def inside_kernel(
    elem_ref, troubled_ref, owner_ref, pos_ref, donor_ref, mean_ref, sec_ref,
    sum_ref, still_ref, far_ref, move_ref, cell_ref, wide_ref,
):
    _, grp, left, right, odd = places()
    own = lax.axis_index("wide") * GROUP + grp
    elem = elem_ref[...]
    troubled = jnp.sum(
        jnp.where(troubled_ref[...] == iota((ELEM, 48), 0), 1.0, 0.0), axis=1, keepdims=True
    )
    local = jnp.where(lax.shift_right_logical(elem, 7) == own, elem & (ELEM - 1), -1)
    rows = iota((ROWS, ELEM), 0)
    elems = iota((ELEM, ELEM), 0)
    near = jnp.where(elems == iota((ELEM, ELEM), 1), 4.0, 0.0)
    far = jnp.zeros((ROWS, ELEM), F32)
    for f in range(FACES):
        near = near + jnp.where(elems == local[f : f + 1, :], 1.0, 0.0)
        far = far + jnp.where(rows == pos_ref[f : f + 1, :], 1.0, 0.0)
    far_ref[...] = jnp.concatenate([far, jnp.zeros((64, ELEM), F32)], axis=0).T[:, :ROWS].astype(BF16)
    sum_ref[...] = select_nt(near.T.astype(BF16), donor_ref[...])
    for v in range(VARS):
        wide_ref[0:NODES, :] = sec_ref[v]
        wide_ref[NODES:128, :] = jnp.zeros((3, ELEM), F32)
        value = wide_ref[...].T
        mean = jnp.broadcast_to(mean_ref[v : v + 1, :], (ELEM, ELEM)).T
        still_ref[:, 128 * v : 128 * v + 128] = jnp.where(troubled > 0.5, mean, value)
    owner = owner_ref[...]
    out0 = jnp.where(odd == 1, left, right)
    out1 = jnp.where(odd == 1, right, left)
    stays = jnp.where(owner == own, 1.0, 0.0)
    cell_ref[:, 0:128] = jnp.broadcast_to(troubled, (ELEM, ELEM))
    cell_ref[:, 128:256] = jnp.broadcast_to(stays, (ELEM, ELEM)).T
    go0 = jnp.where(owner == out0, 1.0, 0.0)
    go1 = jnp.where(owner == out1, 1.0, 0.0)
    go = jnp.concatenate([go0, go1, jnp.zeros((6, ELEM), F32)], axis=0)
    order = dot_nn(go.astype(BF16), strict_upper())
    place = jnp.where(go0 > 0.5, order[0:1, :], jnp.where(go1 > 0.5, MOVE_CAP + order[1:2, :], -1.0))
    move_ref[...] = onehot(iota((2 * MOVE_CAP, ELEM), 0) == place.astype(I32))


def limit_kernel(
    grp_ref, pair0_ref, pair1_ref, sum_ref, still_ref, far_ref, move_ref, cell_ref,
    limited_ref, go0_ref, go1_ref,
):
    got = jnp.concatenate([grp_ref[...], pair0_ref[...], pair1_ref[...]], axis=0)
    hi, mid, lo = thirds(got)
    far = far_ref[...]
    total = sum_ref[...] + (dot_nn(far, hi) + dot_nn(far, mid) + dot_nn(far, lo))
    troubled = cell_ref[:, 0:1] > 0.5
    for v in range(VARS):
        cols = slice(128 * v, 128 * v + 128)
        scale = jnp.where(troubled, 1.0 / total[:, 128 * v + NODES : 128 * v + NODES + 1], 0.0)
        limited_ref[:, cols] = still_ref[:, cols] + scale * total[:, cols]
    hi, mid, lo = thirds(limited_ref[...])
    move = move_ref[...]
    moved = dot_nn(move, hi) + dot_nn(move, mid) + dot_nn(move, lo)
    go0_ref[...] = moved[:MOVE_CAP]
    go1_ref[...] = moved[MOVE_CAP:]


def keep_kernel(limited_ref, cell_ref, out_ref):
    stays = cell_ref[:, 128:256] > 0.5
    for v in range(VARS):
        out_ref[v] = jnp.where(stays, limited_ref[:, 128 * v : 128 * v + 128], 0.0)[:, :NODES]


def arrive_kernel(in0_ref, in1_ref, kept_ref, out_ref):
    odd = lax.rem(lax.axis_index("wide"), 2) == 1
    from_left = jnp.where(odd, in0_ref[...], in1_ref[...])
    from_right = jnp.where(odd, in1_ref[...], in0_ref[...])
    for v in range(VARS):
        out_ref[v, 0:MOVE_CAP, :] = from_left[:, 128 * v : 128 * v + NODES]
        out_ref[v, MOVE_CAP:, :] = from_right[:, 128 * v : 128 * v + NODES]


VMEM = pl.BlockSpec(memory_space=pltpu.VMEM)
PARAMS = pltpu.CompilerParams(vmem_limit_bytes=16 * 1024 * 1024)


def call(kernel, shapes, scratch, *args):
    args = [pltpu.with_memory_space_constraint(arg, pltpu.VMEM) for arg in args]
    return pl.pallas_call(
        kernel,
        out_shape=[pltpu.VMEM(shape, dtype) for shape, dtype in shapes],
        in_specs=[VMEM] * len(args),
        out_specs=[VMEM] * len(shapes),
        scratch_shapes=[pltpu.VMEM(shape, dtype) for shape, dtype in scratch],
        compiler_params=PARAMS,
        interpret=INTERPRET,
    )(*args)


def swap(pair0, pair1):
    size = lax.axis_size("wide")
    first = [(i, i ^ 1) for i in range(size)]
    second = [(i, (i + 1) % size if i % 2 else (i - 1) % size) for i in range(size)]
    got1 = lax.ppermute(pair1, "wide", second)
    got0 = lax.ppermute(pair0, "wide", first)
    return got0, got1


def exchange(blocks, pair0, pair1):
    lanes = blocks.shape[1]
    got = lax.all_to_all(blocks.reshape(GROUP, GROUP_FACES, lanes), "grp", 0, 0)
    return (got.reshape(GROUP_ROWS, lanes), *swap(pair0, pair1))


def shards(state, metric, nbr_elem, nbr_face, troubled, new_owner):
    diffs, weights = gll_tables()
    diff = np.zeros((128, 384), np.float32)
    for a in range(3):
        diff[:NODES, 128 * a : 128 * a + NODES] = diffs[a]
    diff = jnp.asarray(diff)
    weight = jnp.asarray(np.repeat(weights[:, None], ELEM, axis=1), F32)
    metric = metric.reshape(1, ELEM)
    troubled = troubled.reshape(1, 48)
    new_owner = new_owner.reshape(1, ELEM)
    cols = VARS * 128
    wide_lanes = FACES * ELEM

    loaded = [
        pltpu.with_memory_space_constraint(x, pltpu.HBM)
        for x in (nbr_elem, state, nbr_face, metric, troubled, new_owner, diff, weight)
    ]
    blocks, pair0, pair1, trace, pick, nbr_elem, state, nbr_face, metric, troubled, new_owner, diff, weight = pl.pallas_call(
        pack_kernel,
        out_shape=[
            pltpu.VMEM(shape, dtype)
            for shape, dtype in (
                ((GROUP_ROWS, 128), F32), ((32, 128), F32), ((32, 128), F32), ((128, wide_lanes), F32), ((ROWS, ELEM), BF16)
            )
        ]
        + [pltpu.VMEM(x.shape, x.dtype) for x in loaded],
        in_specs=[pl.BlockSpec(memory_space=pltpu.HBM)] * len(loaded),
        out_specs=[VMEM] * (5 + len(loaded)),
        scratch_shapes=[pltpu.VMEM((ROWS, wide_lanes), BF16), pltpu.SemaphoreType.DMA((len(loaded),))],
        compiler_params=PARAMS,
        interpret=INTERPRET,
    )(*loaded)
    got, got0, got1 = exchange(blocks, pair0, pair1)
    base, speeds, near, take, pos = call(
        local_kernel,
        [((VARS, NODES, ELEM), F32), ((FACES, 25, ELEM), F32), ((128, wide_lanes), F32), ((ROWS, wide_lanes), BF16), ((8, ELEM), I32)],
        [((384, cols), F32), ((ELEM, 8), F32)],
        nbr_elem, nbr_face, state, metric, trace, diff,
    )
    blocks, pair0, pair1, sec, donor, mean = call(
        section_kernel,
        [((GROUP_ROWS, cols), F32), ((32, cols), F32), ((32, cols), F32), ((VARS, NODES, ELEM), F32), ((cols, ELEM), F32), ((8, ELEM), F32)],
        [((128, wide_lanes), F32)],
        got, got0, got1, base, speeds, near, take, trace, pick, metric, weight,
    )
    got, got0, got1 = exchange(blocks, pair0, pair1)
    total, still, far, move, cell = call(
        inside_kernel,
        [((ELEM, cols), F32), ((ELEM, cols), F32), ((ELEM, ROWS), BF16), ((2 * MOVE_CAP, ELEM), BF16), ((ELEM, 256), F32)],
        [((128, ELEM), F32)],
        nbr_elem, troubled, new_owner, pos, donor, mean, sec,
    )
    limited, go0, go1 = call(
        limit_kernel,
        [((ELEM, cols), F32), ((MOVE_CAP, cols), F32), ((MOVE_CAP, cols), F32)],
        [],
        got, got0, got1, total, still, far, move, cell,
    )
    in0, in1 = swap(go0, go1)
    out_shape = jax.ShapeDtypeStruct((VARS, ELEM + 2 * MOVE_CAP, NODES), F32)
    vmem = lambda x: pltpu.with_memory_space_constraint(x, pltpu.VMEM)
    kept = pl.pallas_call(
        keep_kernel,
        out_shape=out_shape,
        grid=(1,),
        in_specs=[VMEM, VMEM],
        out_specs=pl.BlockSpec((VARS, ELEM, NODES), lambda i: (0, 0, 0)),
        compiler_params=PARAMS,
        interpret=INTERPRET,
    )(vmem(limited), vmem(cell))
    moved = pl.pallas_call(
        arrive_kernel,
        out_shape=out_shape,
        grid=(1,),
        in_specs=[VMEM, VMEM, pl.BlockSpec(memory_space=pl.ANY)],
        out_specs=pl.BlockSpec((VARS, 2 * MOVE_CAP, NODES), lambda i: (0, 2, 0)),
        input_output_aliases={2: 0},
        compiler_params=PARAMS,
        interpret=INTERPRET,
    )(vmem(in0), vmem(in1), kept)
    return jnp.transpose(moved, (0, 2, 1))


def solution(mesh):
    placed = (
        P(None, None, ("wide", "grp")),
        P(("wide", "grp")),
        P(None, ("wide", "grp")),
        P(None, ("wide", "grp")),
        P(("wide", "grp")),
        P(("wide", "grp")),
    )
    return jax.shard_map(
        shards,
        mesh=mesh,
        in_specs=placed,
        out_specs=P(None, None, ("wide", "grp")),
        check_vma=False,
    )
```

```python
import math

import jax
import jax.numpy as jnp
import numpy as np
from jax import lax
from jax.experimental import pallas as pl
from jax.experimental.pallas import tpu as pltpu
from jax.sharding import PartitionSpec as P


GROUP_FACES = 16
WIDE_FACES = 32
MOVE_CAP = 32
SECTION_STEP = 0.01
LIFT_GAIN = 10.0

ELEM = 128
VARS = 5
NODES = 125
FACES = 6
GROUP = 8
GROUP_ROWS = GROUP * GROUP_FACES
PAIR1 = GROUP_ROWS + WIDE_FACES
ROWS = GROUP_ROWS + 2 * WIDE_FACES
LOCAL = 10

F32 = jnp.float32
BF16 = jnp.bfloat16
I32 = jnp.int32
INTERPRET = False


def gll_tables():
    root = math.sqrt(3.0 / 7.0)
    points = np.array([-1.0, -root, 0.0, root, 1.0])
    weights = np.array([0.1, 49.0 / 90.0, 32.0 / 45.0, 49.0 / 90.0, 0.1])
    bary = np.array(
        [1.0 / np.prod([points[j] - points[k] for k in range(5) if k != j]) for j in range(5)]
    )
    deriv = np.zeros((5, 5))
    for i in range(5):
        for j in range(5):
            if i != j:
                deriv[i, j] = bary[j] / bary[i] / (points[i] - points[j])
        deriv[i, i] = -np.sum(deriv[i])
    ident = np.eye(5)
    diffs = [
        np.kron(np.kron(deriv, ident), ident),
        np.kron(np.kron(ident, deriv), ident),
        np.kron(np.kron(ident, ident), deriv),
    ]
    cell_weights = np.kron(np.kron(weights, weights), weights) / 8.0
    return diffs, cell_weights


def halves_of(table):
    hi = table.astype(jnp.bfloat16)
    return hi, (table - hi.astype(np.float32)).astype(jnp.bfloat16)


def face_rows(face):
    if face < 2:
        return [(100 * face, 25, 1, 0)]
    if face < 4:
        return [(25 * a + 20 * (face - 2), 5, 1, 5 * a) for a in range(5)]
    return [(4 * (face - 4), 25, 5, 0)]


def rows_at(first, count, stride):
    return pl.ds(first, count) if stride == 1 else pl.ds(first, count, stride=stride)


def thirds(x):
    hi = x.astype(BF16)
    rest = x - hi.astype(F32)
    mid = rest.astype(BF16)
    lo = (rest - mid.astype(F32)).astype(BF16)
    return hi, mid, lo


def halves(x):
    hi = x.astype(BF16)
    return hi, (x - hi.astype(F32)).astype(BF16)


def dot_nn(a, b):
    return lax.dot_general(a, b, (((1,), (0,)), ((), ())), preferred_element_type=F32)


def dot_nt(a, b):
    return lax.dot_general(a, b, (((1,), (1,)), ((), ())), preferred_element_type=F32)


def select_nt(onehot, values):
    hi, mid, lo = thirds(values)
    return dot_nt(onehot, hi) + dot_nt(onehot, mid) + dot_nt(onehot, lo)


def iota(shape, dim):
    return lax.broadcasted_iota(I32, shape, dim)


def onehot(mask):
    return jnp.where(mask, 1.0, 0.0).astype(BF16)


def places():
    wide = lax.axis_index("wide")
    grp = lax.axis_index("grp")
    size = lax.axis_size("wide")
    left = lax.rem(wide + size - 1, size) * GROUP + grp
    right = lax.rem(wide + 1, size) * GROUP + grp
    odd = lax.rem(wide, 2)
    return wide, grp, left, right, odd


def categories(nbr_elem):
    wide, grp, left, _, odd = places()
    owner = lax.shift_right_logical(nbr_elem, 7)
    beside = jnp.where(owner == left, 9 - odd, 8 + odd)
    cat = jnp.where(lax.shift_right_logical(owner, 3) == wide, owner & 7, beside)
    return jnp.where(owner == wide * GROUP + grp, LOCAL, cat)


def strict_upper():
    return onehot(iota((ELEM, ELEM), 0) < iota((ELEM, ELEM), 1))


def pack_kernel(
    elem_hbm, face_hbm, state_hbm, metric_hbm, troubled_hbm, owner_hbm, diff_hbm, weight_hbm,
    grp_hbm, pair0_ref, pair1_ref, trace_ref, pick_ref,
    elem_ref, face_ref, state_ref, metric_ref, troubled_ref, owner_ref, diff_ref, weight_ref,
    s_ref, grp_ref, sems,
):
    pairs = [(elem_hbm, elem_ref), (face_hbm, face_ref)]
    pairs += [(state_hbm.at[v], state_ref.at[v]) for v in range(VARS)]
    pairs += [(metric_hbm, metric_ref), (troubled_hbm, troubled_ref), (owner_hbm, owner_ref)]
    pairs += [(diff_hbm, diff_ref), (weight_hbm, weight_ref)]
    copies = [pltpu.make_async_copy(x, y, sems.at[k]) for k, (x, y) in enumerate(pairs)]
    for copy in copies:
        copy.start()
    copies[0].wait()
    copies[1].wait()
    elem = elem_ref[...]
    cat = categories(elem)
    partner = face_ref[...] * ELEM + (elem & (ELEM - 1)) + 1
    kinds = iota((16, ELEM), 0)
    hot = [jnp.where(cat[f : f + 1, :] == kinds, 1.0, 0.0) for f in range(FACES)]
    upper = jnp.concatenate([strict_upper(), jnp.ones((ELEM, ELEM), BF16)], axis=1)
    counts = dot_nn(jnp.concatenate(hot, axis=0).astype(BF16), upper)
    base = jnp.where(kinds < 9, 16 * kinds, PAIR1).astype(F32)
    pick = jnp.zeros((ROWS, ELEM), F32)
    rows = iota((ROWS, ELEM), 0)
    trace_ref[126:128, :] = jnp.zeros((2, FACES * ELEM), F32)
    for f in range(FACES):
        part = counts[16 * f : 16 * f + 16]
        pos = jnp.sum(hot[f] * (part[:, :ELEM] + base), axis=0, keepdims=True)
        base = base + part[:, ELEM:]
        pos = jnp.where(cat[f : f + 1, :] == LOCAL, -1, pos.astype(I32))
        chosen = jnp.where(rows == pos, 1.0, 0.0)
        pick = pick + chosen
        s_ref[:, f * ELEM : (f + 1) * ELEM] = chosen.astype(BF16)
        trace_ref[125:126, f * ELEM : (f + 1) * ELEM] = partner[f : f + 1, :].astype(F32)
    pick_ref[...] = pick.astype(BF16)
    for v in range(VARS):
        copies[2 + v].wait()
        for f in range(FACES):
            for first, count, stride, place in face_rows(f):
                trace_ref[25 * v + place : 25 * v + place + count, f * ELEM : (f + 1) * ELEM] = state_ref[
                    v, rows_at(first, count, stride), :
                ]
    pieces = thirds(trace_ref[...])
    grp_ref[...] = sum(dot_nt(s_ref[:GROUP_ROWS], x) for x in pieces)
    send = pltpu.make_async_copy(grp_ref, grp_hbm, sems.at[len(copies)])
    send.start()
    sent = sum(dot_nt(s_ref[GROUP_ROWS:], x) for x in pieces)
    pair0_ref[...] = sent[:WIDE_FACES]
    pair1_ref[...] = sent[WIDE_FACES:]
    for copy in copies[2 + VARS :]:
        copy.wait()
    send.wait()


def primitives(u):
    inv = 1.0 / u[0]
    vel = [u[1] * inv, u[2] * inv, u[3] * inv]
    kinetic = u[1] * vel[0] + u[2] * vel[1] + u[3] * vel[2]
    pressure = 0.4 * (u[4] - 0.5 * kinetic)
    return inv, vel, pressure


def flux(u, vel, pressure, a):
    w = vel[a]
    rows = [u[1 + a], u[1] * w, u[2] * w, u[3] * w, (u[4] + pressure) * w]
    rows[1 + a] = rows[1 + a] + pressure
    return rows


def speed(inv, vel, pressure, a):
    return jnp.abs(vel[a]) + jnp.sqrt(1.4 * pressure * inv)


def face_values(ref, f):
    return [ref[25 * v : 25 * v + 25, f * ELEM : (f + 1) * ELEM] for v in range(VARS)]


def add_face(ref, f, v, value):
    for first, count, stride, place in face_rows(f):
        at = rows_at(first, count, stride)
        ref[v, at, :] = ref[v, at, :] + value[place : place + count]


def local_kernel(
    elem_ref, face_ref, state_ref, metric_ref, trace_ref, diff_ref,
    base_ref, speed_ref, near_ref, f_ref, volume_ref,
):
    metric = metric_ref[...]
    u = [state_ref[v] for v in range(VARS)]
    inv, vel, pressure = primitives(u)
    for a in range(3):
        for v, row in enumerate(flux(u, vel, pressure, a)):
            f_ref[128 * a : 128 * a + NODES, v * ELEM : (v + 1) * ELEM] = row
        f_ref[128 * a + NODES : 128 * a + 128, :] = jnp.zeros((3, VARS * ELEM), F32)
    hi, mid = halves(f_ref[...])
    wide = dot_nn(diff_ref[...], hi)
    volume_ref[...] = wide[:128] + wide[128:] + dot_nn(diff_ref[0:128, :], mid)
    for v in range(VARS):
        base_ref[v] = state_ref[v]
    elem = elem_ref[...]
    _, grp, _, _, _ = places()
    own = lax.axis_index("wide") * GROUP + grp
    here = lax.shift_right_logical(elem, 7) == own
    local = elem & (ELEM - 1)
    side = face_ref[...]
    at = [jnp.where(here & (side == g), local, -1).astype(F32).astype(BF16) for g in range(FACES)]
    elems = iota((ELEM, 2 * ELEM), 0).astype(F32).astype(BF16)
    one, zero = jnp.ones((), BF16), jnp.zeros((), BF16)
    stacked = jnp.concatenate(halves(trace_ref[...]), axis=0)
    half = (0.5 * LIFT_GAIN * SECTION_STEP) * metric
    for pair in range(3):
        blocks = []
        for g in range(FACES):
            row = jnp.concatenate([at[g][2 * pair : 2 * pair + 1], at[g][2 * pair + 1 : 2 * pair + 2]], axis=1)
            blocks.append(jnp.where(elems == row, one, zero))
        got = dot_nn(stacked, jnp.concatenate(blocks, axis=0))
        near_ref[:, 2 * pair * ELEM : 2 * (pair + 1) * ELEM] = got[:128] + got[128:]
        for f in (2 * pair, 2 * pair + 1):
            scale = half if f % 2 else -half
            inner = face_values(trace_ref, f)
            inv, vel, pressure = primitives(inner)
            speed_ref[f] = speed(inv, vel, pressure, pair)
            for v, row in enumerate(flux(inner, vel, pressure, pair)):
                add_face(base_ref, f, v, scale * row)
    for v in range(VARS):
        base_ref[v] = base_ref[v] - (SECTION_STEP * metric) * volume_ref[:NODES, v * ELEM : (v + 1) * ELEM]


def section_kernel(
    grp_ref, pair0_ref, pair1_ref, base_ref, speed_ref, near_ref, trace_ref, pick_ref, metric_ref, weight_ref,
    send_hbm, send0_ref, send1_ref, sec_ref, donor_ref, mean_ref, came_ref, outer_ref, send_ref, sem,
):
    got = jnp.concatenate([grp_ref[...], pair0_ref[...], pair1_ref[...]], axis=0)
    slot = jnp.broadcast_to(got[:, NODES : NODES + 1], (ROWS, ELEM))
    lanes = iota((1, ELEM), 1).astype(F32) + 1.0
    stacked = jnp.concatenate(halves(got.T), axis=0)
    for pair in range(3):
        takes = [jnp.where(slot == lanes + float(f * ELEM), 1.0, 0.0) for f in (2 * pair, 2 * pair + 1)]
        far = dot_nn(stacked, jnp.concatenate(takes, axis=1).astype(BF16))
        cols = slice(2 * pair * ELEM, 2 * (pair + 1) * ELEM)
        outer_ref[:, cols] = near_ref[:, cols] + far[:128] + far[128:]
    came_ref[...] = slot
    half = (0.5 * LIFT_GAIN * SECTION_STEP) * metric_ref[...]
    sec_ref[...] = base_ref[...]
    for f in range(FACES):
        a = f // 2
        sign = 1.0 if f % 2 else -1.0
        inner = face_values(trace_ref, f)
        outer = face_values(outer_ref, f)
        inv, vel, pressure = primitives(outer)
        lam = half * jnp.maximum(speed_ref[f], speed(inv, vel, pressure, a))
        for v, row in enumerate(flux(outer, vel, pressure, a)):
            add_face(sec_ref, f, v, lam * (outer[v] - inner[v]) - (sign * half) * row)
    weight = weight_ref[...]
    for v in range(VARS):
        q = sec_ref[v]
        mean = jnp.sum(weight * q, axis=0, keepdims=True)
        dev = q - mean
        beta = 1e-06 + jnp.sum(weight * dev * dev, axis=0, keepdims=True)
        omega = 0.1 / (beta * beta)
        donor_ref[128 * v : 128 * v + NODES, :] = omega * dev
        donor_ref[128 * v + NODES : 128 * v + NODES + 1, :] = omega
        donor_ref[128 * v + NODES + 1 : 128 * v + 128, :] = jnp.zeros((2, ELEM), F32)
        mean_ref[v : v + 1, :] = mean
    pieces = thirds(donor_ref[...])
    send_ref[...] = sum(dot_nt(pick_ref[:GROUP_ROWS], x) for x in pieces)
    send = pltpu.make_async_copy(send_ref, send_hbm, sem.at[0])
    send.start()
    sent = sum(dot_nt(pick_ref[GROUP_ROWS:], x) for x in pieces)
    send0_ref[...] = sent[:WIDE_FACES]
    send1_ref[...] = sent[WIDE_FACES:]
    send.wait()


def inside_kernel(
    elem_ref, troubled_ref, owner_ref, came_ref, donor_ref, mean_ref, sec_ref,
    sum_ref, still_ref, far_ref, move_ref, cell_ref, wide_ref,
):
    _, grp, left, right, odd = places()
    own = lax.axis_index("wide") * GROUP + grp
    elem = elem_ref[...]
    troubled = jnp.sum(
        jnp.where(troubled_ref[...] == iota((ELEM, 48), 0), 1.0, 0.0), axis=1, keepdims=True
    )
    local = jnp.where(lax.shift_right_logical(elem, 7) == own, elem & (ELEM - 1), -1)
    elems = iota((ELEM, ELEM), 0)
    near = jnp.where(elems == iota((ELEM, ELEM), 1), 4.0, 0.0)
    for f in range(FACES):
        near = near + jnp.where(elems == local[f : f + 1, :], 1.0, 0.0)
    slot = came_ref[...].astype(I32) - 1
    came = jnp.where((slot & (ELEM - 1)) == jnp.where(slot < 0, -1, iota((ROWS, ELEM), 1)), 1.0, 0.0)
    far_ref[...] = jnp.concatenate([came, jnp.zeros((64, ELEM), F32)], axis=0).T[:, :ROWS].astype(BF16)
    sum_ref[...] = select_nt(near.T.astype(BF16), donor_ref[...])
    for v in range(VARS):
        wide_ref[0:NODES, :] = sec_ref[v]
        wide_ref[NODES:128, :] = jnp.zeros((3, ELEM), F32)
        value = wide_ref[...].T
        mean = jnp.broadcast_to(mean_ref[v : v + 1, :], (ELEM, ELEM)).T
        still_ref[:, 128 * v : 128 * v + 128] = jnp.where(troubled > 0.5, mean, value)
    owner = owner_ref[...]
    out0 = jnp.where(odd == 1, left, right)
    out1 = jnp.where(odd == 1, right, left)
    stays = jnp.where(owner == own, 1.0, 0.0)
    cell_ref[:, 0:128] = jnp.broadcast_to(troubled, (ELEM, ELEM))
    cell_ref[:, 128:256] = jnp.broadcast_to(stays, (ELEM, ELEM)).T
    go0 = jnp.where(owner == out0, 1.0, 0.0)
    go1 = jnp.where(owner == out1, 1.0, 0.0)
    go = jnp.concatenate([go0, go1, jnp.zeros((6, ELEM), F32)], axis=0)
    order = dot_nn(go.astype(BF16), strict_upper())
    place = jnp.where(go0 > 0.5, order[0:1, :], jnp.where(go1 > 0.5, MOVE_CAP + order[1:2, :], -1.0))
    move_ref[...] = onehot(iota((2 * MOVE_CAP, ELEM), 0) == place.astype(I32))


def limit_kernel(
    grp_ref, pair0_ref, pair1_ref, sum_ref, still_ref, far_ref, move_ref, cell_ref,
    limited_ref, go0_ref, go1_ref,
):
    got = jnp.concatenate([grp_ref[...], pair0_ref[...], pair1_ref[...]], axis=0)
    hi, mid = halves(got)
    far = far_ref[...]
    total = sum_ref[...] + (dot_nn(far, hi) + dot_nn(far, mid))
    troubled = cell_ref[:, 0:1] > 0.5
    for v in range(VARS):
        cols = slice(128 * v, 128 * v + 128)
        scale = jnp.where(troubled, 1.0 / total[:, 128 * v + NODES : 128 * v + NODES + 1], 0.0)
        limited_ref[:, cols] = still_ref[:, cols] + scale * total[:, cols]
    hi, mid, lo = thirds(limited_ref[...])
    move = move_ref[...]
    moved = dot_nn(move, hi) + dot_nn(move, mid) + dot_nn(move, lo)
    for v in range(VARS):
        go0_ref[v] = moved[:MOVE_CAP, 128 * v : 128 * v + NODES]
        go1_ref[v] = moved[MOVE_CAP:, 128 * v : 128 * v + NODES]


def keep_kernel(limited_ref, cell_ref, out_ref):
    stays = cell_ref[:, 128:256] > 0.5
    for v in range(VARS):
        out_ref[v] = jnp.where(stays, limited_ref[:, 128 * v : 128 * v + 128], 0.0)[:, :NODES]


def arrive_kernel(in0_ref, in1_ref, kept_ref, out_ref, sems):
    odd = lax.rem(lax.axis_index("wide"), 2)
    copies = []
    for k, (ref, place) in enumerate(((in0_ref, 1 - odd), (in1_ref, odd))):
        at = pl.ds(pl.multiple_of(ELEM + MOVE_CAP * place, 32), MOVE_CAP)
        copies.append(pltpu.make_async_copy(ref, out_ref.at[:, at, :], sems.at[k]))
    for copy in copies:
        copy.start()
    for copy in copies:
        copy.wait()


VMEM = pl.BlockSpec(memory_space=pltpu.VMEM)
PARAMS = pltpu.CompilerParams(vmem_limit_bytes=16 * 1024 * 1024)


def call(kernel, shapes, scratch, args, hbm=(), to_hbm=0):
    inputs = [pltpu.with_memory_space_constraint(arg, pltpu.VMEM) for arg in args]
    inputs += [pltpu.with_memory_space_constraint(arg, pltpu.HBM) for arg in hbm]
    spaces = [pltpu.HBM] * to_hbm + [pltpu.VMEM] * (len(shapes) - to_hbm)
    return pl.pallas_call(
        kernel,
        out_shape=[space(shape, dtype) for space, (shape, dtype) in zip(spaces, shapes)],
        in_specs=[VMEM] * len(args) + [pl.BlockSpec(memory_space=pltpu.HBM)] * len(hbm),
        out_specs=[pl.BlockSpec(memory_space=space) for space in spaces],
        scratch_shapes=scratch,
        compiler_params=PARAMS,
        interpret=INTERPRET,
    )(*inputs)


def swap(pair0, pair1):
    size = lax.axis_size("wide")
    first = [(i, i ^ 1) for i in range(size)]
    second = [(i, (i + 1) % size if i % 2 else (i - 1) % size) for i in range(size)]
    got1 = lax.ppermute(pair1, "wide", second)
    got0 = lax.ppermute(pair0, "wide", first)
    return got0, got1


def exchange(blocks, pair0, pair1):
    lanes = blocks.shape[1]
    got = lax.all_to_all(blocks.reshape(GROUP, GROUP_FACES, lanes), "grp", 0, 0)
    return (got.reshape(GROUP_ROWS, lanes), *swap(pair0, pair1))


def shards(state, metric, nbr_elem, nbr_face, troubled, new_owner):
    diffs, weights = gll_tables()
    diff = np.zeros((128, 384), np.float32)
    for a in range(3):
        diff[:NODES, 128 * a : 128 * a + NODES] = diffs[a]
    diff = jnp.asarray(np.concatenate(halves_of(diff), axis=0))
    weight = jnp.asarray(np.repeat(weights[:, None], ELEM, axis=1), F32)
    metric = metric.reshape(1, ELEM)
    troubled = troubled.reshape(1, 48)
    new_owner = new_owner.reshape(1, ELEM)
    cols = VARS * 128
    slots = FACES * ELEM
    dma = pltpu.SemaphoreType.DMA

    loaded = (nbr_elem, nbr_face, state, metric, troubled, new_owner, diff, weight)
    blocks, pair0, pair1, trace, pick, nbr_elem, nbr_face, state, metric, troubled, new_owner, diff, weight = call(
        pack_kernel,
        [((GROUP_ROWS, 128), F32), ((32, 128), F32), ((32, 128), F32), ((128, slots), F32), ((ROWS, ELEM), BF16)]
        + [(x.shape, x.dtype) for x in loaded],
        [pltpu.VMEM((ROWS, slots), BF16), pltpu.VMEM((GROUP_ROWS, 128), F32), dma((8 + VARS,))],
        (), loaded, 1,
    )
    got, got0, got1 = exchange(blocks, pair0, pair1)
    base, speeds, near = call(
        local_kernel,
        [((VARS, NODES, ELEM), F32), ((FACES, 25, ELEM), F32), ((128, slots), F32)],
        [pltpu.VMEM((384, cols), F32), pltpu.VMEM((128, cols), F32)],
        (nbr_elem, nbr_face, state, metric, trace, diff),
    )
    blocks, pair0, pair1, sec, donor, mean, came = call(
        section_kernel,
        [((GROUP_ROWS, cols), F32), ((32, cols), F32), ((32, cols), F32), ((VARS, NODES, ELEM), F32),
         ((cols, ELEM), F32), ((8, ELEM), F32), ((ROWS, ELEM), F32)],
        [pltpu.VMEM((128, slots), F32), pltpu.VMEM((GROUP_ROWS, cols), F32), dma((1,))],
        (got, got0, got1, base, speeds, near, trace, pick, metric, weight), (), 1,
    )
    got, got0, got1 = exchange(blocks, pair0, pair1)
    total, still, far, move, cell = call(
        inside_kernel,
        [((ELEM, cols), F32), ((ELEM, cols), F32), ((ELEM, ROWS), BF16), ((2 * MOVE_CAP, ELEM), BF16), ((ELEM, 256), F32)],
        [pltpu.VMEM((128, ELEM), F32)],
        (nbr_elem, troubled, new_owner, came, donor, mean, sec),
    )
    limited, go0, go1 = call(
        limit_kernel,
        [((ELEM, cols), F32), ((VARS, MOVE_CAP, NODES), F32), ((VARS, MOVE_CAP, NODES), F32)],
        [],
        (got, got0, got1, total, still, far, move, cell),
    )
    in0, in1 = swap(go0, go1)
    out_shape = jax.ShapeDtypeStruct((VARS, ELEM + 2 * MOVE_CAP, NODES), F32)
    vmem = lambda x: pltpu.with_memory_space_constraint(x, pltpu.VMEM)
    kept = pl.pallas_call(
        keep_kernel,
        out_shape=out_shape,
        grid=(1,),
        in_specs=[VMEM, VMEM],
        out_specs=pl.BlockSpec((VARS, ELEM, NODES), lambda i: (0, 0, 0)),
        compiler_params=PARAMS,
        interpret=INTERPRET,
    )(vmem(limited), vmem(cell))
    moved = pl.pallas_call(
        arrive_kernel,
        out_shape=out_shape,
        in_specs=[VMEM, VMEM, pl.BlockSpec(memory_space=pl.ANY)],
        out_specs=pl.BlockSpec(memory_space=pl.ANY),
        input_output_aliases={2: 0},
        scratch_shapes=[dma((2,))],
        compiler_params=PARAMS,
        interpret=INTERPRET,
    )(vmem(in0), vmem(in1), kept)
    return jnp.transpose(moved, (0, 2, 1))


def solution(mesh):
    placed = (
        P(None, None, ("wide", "grp")),
        P(("wide", "grp")),
        P(None, ("wide", "grp")),
        P(None, ("wide", "grp")),
        P(("wide", "grp")),
        P(("wide", "grp")),
    )
    return jax.shard_map(
        shards,
        mesh=mesh,
        in_specs=placed,
        out_specs=P(None, None, ("wide", "grp")),
        check_vma=False,
    )
```

```python
import math

import jax
import jax.numpy as jnp
import numpy as np
from jax import lax
from jax.experimental import pallas as pl
from jax.experimental.pallas import tpu as pltpu
from jax.sharding import PartitionSpec as P


GROUP_FACES = 16
WIDE_FACES = 32
MOVE_CAP = 32
SECTION_STEP = 0.01
LIFT_GAIN = 10.0

ELEM = 128
VARS = 5
NODES = 125
FACES = 6
GROUP = 8
GROUP_ROWS = GROUP * GROUP_FACES
PAIR1 = GROUP_ROWS + WIDE_FACES
ROWS = GROUP_ROWS + 2 * WIDE_FACES
LOCAL = 10

F32 = jnp.float32
BF16 = jnp.bfloat16
I32 = jnp.int32
INTERPRET = False


def gll_tables():
    root = math.sqrt(3.0 / 7.0)
    points = np.array([-1.0, -root, 0.0, root, 1.0])
    weights = np.array([0.1, 49.0 / 90.0, 32.0 / 45.0, 49.0 / 90.0, 0.1])
    bary = np.array(
        [1.0 / np.prod([points[j] - points[k] for k in range(5) if k != j]) for j in range(5)]
    )
    deriv = np.zeros((5, 5))
    for i in range(5):
        for j in range(5):
            if i != j:
                deriv[i, j] = bary[j] / bary[i] / (points[i] - points[j])
        deriv[i, i] = -np.sum(deriv[i])
    ident = np.eye(5)
    diffs = [
        np.kron(np.kron(deriv, ident), ident),
        np.kron(np.kron(ident, deriv), ident),
        np.kron(np.kron(ident, ident), deriv),
    ]
    cell_weights = np.kron(np.kron(weights, weights), weights) / 8.0
    return diffs, cell_weights


def halves_of(table):
    hi = table.astype(jnp.bfloat16)
    return hi, (table - hi.astype(np.float32)).astype(jnp.bfloat16)


def face_rows(face):
    if face < 2:
        return [(100 * face, 25, 1, 0)]
    if face < 4:
        return [(25 * a + 20 * (face - 2), 5, 1, 5 * a) for a in range(5)]
    return [(4 * (face - 4), 25, 5, 0)]


def rows_at(first, count, stride):
    return pl.ds(first, count) if stride == 1 else pl.ds(first, count, stride=stride)


def thirds(x):
    hi = x.astype(BF16)
    rest = x - hi.astype(F32)
    mid = rest.astype(BF16)
    lo = (rest - mid.astype(F32)).astype(BF16)
    return hi, mid, lo


def halves(x):
    hi = x.astype(BF16)
    return hi, (x - hi.astype(F32)).astype(BF16)


def dot_nn(a, b):
    return lax.dot_general(a, b, (((1,), (0,)), ((), ())), preferred_element_type=F32)


def dot_nt(a, b):
    return lax.dot_general(a, b, (((1,), (1,)), ((), ())), preferred_element_type=F32)


def select_nt(onehot, values):
    hi, mid, lo = thirds(values)
    return dot_nt(onehot, hi) + dot_nt(onehot, mid) + dot_nt(onehot, lo)


def iota(shape, dim):
    return lax.broadcasted_iota(I32, shape, dim)


def onehot(mask):
    return jnp.where(mask, 1.0, 0.0).astype(BF16)


def places():
    wide = lax.axis_index("wide")
    grp = lax.axis_index("grp")
    size = lax.axis_size("wide")
    left = lax.rem(wide + size - 1, size) * GROUP + grp
    right = lax.rem(wide + 1, size) * GROUP + grp
    odd = lax.rem(wide, 2)
    return wide, grp, left, right, odd


def categories(nbr_elem):
    wide, grp, left, _, odd = places()
    owner = lax.shift_right_logical(nbr_elem, 7)
    beside = jnp.where(owner == left, 9 - odd, 8 + odd)
    cat = jnp.where(lax.shift_right_logical(owner, 3) == wide, owner & 7, beside)
    return jnp.where(owner == wide * GROUP + grp, LOCAL, cat)


def strict_upper():
    return onehot(iota((ELEM, ELEM), 0) < iota((ELEM, ELEM), 1))


def pack_kernel(
    elem_hbm, face_hbm, state_hbm, metric_hbm, troubled_hbm, owner_hbm, diff_hbm, weight_hbm,
    grp_hbm, pair0_ref, pair1_ref, trace_ref, pick_ref, base_ref,
    elem_ref, face_ref, metric_ref, troubled_ref, owner_ref, weight_ref,
    state_ref, diff_ref, s_ref, grp_ref, f_ref, sems,
):
    pairs = [(elem_hbm, elem_ref), (face_hbm, face_ref)]
    pairs += [(state_hbm.at[v], state_ref.at[v]) for v in range(VARS)]
    pairs += [(metric_hbm, metric_ref), (troubled_hbm, troubled_ref), (owner_hbm, owner_ref)]
    pairs += [(diff_hbm, diff_ref), (weight_hbm, weight_ref)]
    copies = [pltpu.make_async_copy(x, y, sems.at[k]) for k, (x, y) in enumerate(pairs)]
    for copy in copies:
        copy.start()
    copies[0].wait()
    copies[1].wait()
    elem = elem_ref[...]
    cat = categories(elem)
    partner = face_ref[...] * ELEM + (elem & (ELEM - 1)) + 1
    kinds = iota((16, ELEM), 0)
    hot = [jnp.where(cat[f : f + 1, :] == kinds, 1.0, 0.0) for f in range(FACES)]
    upper = jnp.concatenate([strict_upper(), jnp.ones((ELEM, ELEM), BF16)], axis=1)
    counts = dot_nn(jnp.concatenate(hot, axis=0).astype(BF16), upper)
    base = jnp.where(kinds < 9, 16 * kinds, PAIR1).astype(F32)
    pick = jnp.zeros((ROWS, ELEM), F32)
    rows = iota((ROWS, ELEM), 0)
    trace_ref[126:128, :] = jnp.zeros((2, FACES * ELEM), F32)
    for f in range(FACES):
        part = counts[16 * f : 16 * f + 16]
        pos = jnp.sum(hot[f] * (part[:, :ELEM] + base), axis=0, keepdims=True)
        base = base + part[:, ELEM:]
        pos = jnp.where(cat[f : f + 1, :] == LOCAL, -1, pos.astype(I32))
        chosen = jnp.where(rows == pos, 1.0, 0.0)
        pick = pick + chosen
        s_ref[:, f * ELEM : (f + 1) * ELEM] = chosen.astype(BF16)
        trace_ref[125:126, f * ELEM : (f + 1) * ELEM] = partner[f : f + 1, :].astype(F32)
    pick_ref[...] = pick.astype(BF16)
    for v in range(VARS):
        copies[2 + v].wait()
        for f in range(FACES):
            for first, count, stride, place in face_rows(f):
                trace_ref[25 * v + place : 25 * v + place + count, f * ELEM : (f + 1) * ELEM] = state_ref[
                    v, rows_at(first, count, stride), :
                ]
    pieces = halves(trace_ref[...])
    grp_ref[...] = sum(dot_nt(s_ref[:GROUP_ROWS], x) for x in pieces)
    send = pltpu.make_async_copy(grp_ref, grp_hbm, sems.at[len(copies)])
    send.start()
    sent = sum(dot_nt(s_ref[GROUP_ROWS:], x) for x in pieces)
    pair0_ref[...] = sent[:WIDE_FACES]
    pair1_ref[...] = sent[WIDE_FACES:]
    u = [state_ref[v] for v in range(VARS)]
    _, vel, pressure = primitives(u)
    for a in range(3):
        for v, row in enumerate(flux(u, vel, pressure, a)):
            f_ref[128 * a : 128 * a + NODES, v * ELEM : (v + 1) * ELEM] = row
        f_ref[128 * a + NODES : 128 * a + 128, :] = jnp.zeros((3, VARS * ELEM), F32)
    hi, mid = halves(f_ref[...])
    for copy in copies[2 + VARS :]:
        copy.wait()
    wide = dot_nn(diff_ref[...], hi)
    volume = wide[:128] + wide[128:] + dot_nn(diff_ref[0:128, :], mid)
    step = SECTION_STEP * metric_ref[...]
    for v in range(VARS):
        base_ref[v] = state_ref[v] - step * volume[:NODES, v * ELEM : (v + 1) * ELEM]
    send.wait()


def primitives(u):
    inv = 1.0 / u[0]
    vel = [u[1] * inv, u[2] * inv, u[3] * inv]
    kinetic = u[1] * vel[0] + u[2] * vel[1] + u[3] * vel[2]
    pressure = 0.4 * (u[4] - 0.5 * kinetic)
    return inv, vel, pressure


def flux(u, vel, pressure, a):
    w = vel[a]
    rows = [u[1 + a], u[1] * w, u[2] * w, u[3] * w, (u[4] + pressure) * w]
    rows[1 + a] = rows[1 + a] + pressure
    return rows


def speed(inv, vel, pressure, a):
    return jnp.abs(vel[a]) + jnp.sqrt(1.4 * pressure * inv)


def face_values(ref, f):
    return [ref[25 * v : 25 * v + 25, f * ELEM : (f + 1) * ELEM] for v in range(VARS)]


def add_face(ref, f, v, value):
    for first, count, stride, place in face_rows(f):
        at = rows_at(first, count, stride)
        ref[v, at, :] = ref[v, at, :] + value[place : place + count]


def local_kernel(
    elem_ref, face_ref, start_ref, metric_ref, trace_ref,
    base_ref, speed_ref, near_ref,
):
    metric = metric_ref[...]
    for v in range(VARS):
        base_ref[v] = start_ref[v]
    elem = elem_ref[...]
    _, grp, _, _, _ = places()
    own = lax.axis_index("wide") * GROUP + grp
    here = lax.shift_right_logical(elem, 7) == own
    local = elem & (ELEM - 1)
    side = face_ref[...]
    at = [jnp.where(here & (side == g), local, -1).astype(F32).astype(BF16) for g in range(FACES)]
    elems = iota((ELEM, 2 * ELEM), 0).astype(F32).astype(BF16)
    one, zero = jnp.ones((), BF16), jnp.zeros((), BF16)
    stacked = jnp.concatenate(halves(trace_ref[...]), axis=0)
    half = (0.5 * LIFT_GAIN * SECTION_STEP) * metric
    for pair in range(3):
        blocks = []
        for g in range(FACES):
            row = jnp.concatenate([at[g][2 * pair : 2 * pair + 1], at[g][2 * pair + 1 : 2 * pair + 2]], axis=1)
            blocks.append(jnp.where(elems == row, one, zero))
        got = dot_nn(stacked, jnp.concatenate(blocks, axis=0))
        near_ref[:, 2 * pair * ELEM : 2 * (pair + 1) * ELEM] = got[:128] + got[128:]
        for f in (2 * pair, 2 * pair + 1):
            scale = half if f % 2 else -half
            inner = face_values(trace_ref, f)
            inv, vel, pressure = primitives(inner)
            speed_ref[f] = speed(inv, vel, pressure, pair)
            for v, row in enumerate(flux(inner, vel, pressure, pair)):
                add_face(base_ref, f, v, scale * row)


def section_kernel(
    grp_ref, pair0_ref, pair1_ref, base_ref, speed_ref, near_ref, trace_ref, pick_ref, metric_ref, weight_ref,
    send_hbm, send0_ref, send1_ref, sec_ref, donor_ref, mean_ref, came_ref, outer_ref, send_ref, sem,
):
    got = jnp.concatenate([grp_ref[...], pair0_ref[...], pair1_ref[...]], axis=0)
    slot = jnp.broadcast_to(got[:, NODES : NODES + 1], (ROWS, ELEM))
    lanes = iota((1, ELEM), 1).astype(F32) + 1.0
    stacked = jnp.concatenate(halves(got.T), axis=0)
    for pair in range(3):
        takes = [jnp.where(slot == lanes + float(f * ELEM), 1.0, 0.0) for f in (2 * pair, 2 * pair + 1)]
        far = dot_nn(stacked, jnp.concatenate(takes, axis=1).astype(BF16))
        cols = slice(2 * pair * ELEM, 2 * (pair + 1) * ELEM)
        outer_ref[:, cols] = near_ref[:, cols] + far[:128] + far[128:]
    came_ref[...] = slot
    half = (0.5 * LIFT_GAIN * SECTION_STEP) * metric_ref[...]
    sec_ref[...] = base_ref[...]
    for f in range(FACES):
        a = f // 2
        sign = 1.0 if f % 2 else -1.0
        inner = face_values(trace_ref, f)
        outer = face_values(outer_ref, f)
        inv, vel, pressure = primitives(outer)
        lam = half * jnp.maximum(speed_ref[f], speed(inv, vel, pressure, a))
        for v, row in enumerate(flux(outer, vel, pressure, a)):
            add_face(sec_ref, f, v, lam * (outer[v] - inner[v]) - (sign * half) * row)
    weight = weight_ref[...]
    for v in range(VARS):
        q = sec_ref[v]
        mean = jnp.sum(weight * q, axis=0, keepdims=True)
        dev = q - mean
        beta = 1e-06 + jnp.sum(weight * dev * dev, axis=0, keepdims=True)
        omega = 0.1 / (beta * beta)
        donor_ref[128 * v : 128 * v + NODES, :] = omega * dev
        donor_ref[128 * v + NODES : 128 * v + NODES + 1, :] = omega
        donor_ref[128 * v + NODES + 1 : 128 * v + 128, :] = jnp.zeros((2, ELEM), F32)
        mean_ref[v : v + 1, :] = mean
    pieces = halves(donor_ref[...])
    send_ref[...] = sum(dot_nt(pick_ref[:GROUP_ROWS], x) for x in pieces)
    send = pltpu.make_async_copy(send_ref, send_hbm, sem.at[0])
    send.start()
    sent = sum(dot_nt(pick_ref[GROUP_ROWS:], x) for x in pieces)
    send0_ref[...] = sent[:WIDE_FACES]
    send1_ref[...] = sent[WIDE_FACES:]
    send.wait()


def inside_kernel(
    elem_ref, troubled_ref, owner_ref, came_ref, donor_ref, mean_ref, sec_ref,
    sum_ref, still_ref, far_ref, move_ref, cell_ref, wide_ref,
):
    _, grp, left, right, odd = places()
    own = lax.axis_index("wide") * GROUP + grp
    elem = elem_ref[...]
    troubled = jnp.sum(
        jnp.where(troubled_ref[...] == iota((ELEM, 48), 0), 1.0, 0.0), axis=1, keepdims=True
    )
    local = jnp.where(lax.shift_right_logical(elem, 7) == own, elem & (ELEM - 1), -1)
    elems = iota((ELEM, ELEM), 0)
    near = jnp.where(elems == iota((ELEM, ELEM), 1), 4.0, 0.0)
    for f in range(FACES):
        near = near + jnp.where(elems == local[f : f + 1, :], 1.0, 0.0)
    slot = came_ref[...].astype(I32) - 1
    came = jnp.where((slot & (ELEM - 1)) == jnp.where(slot < 0, -1, iota((ROWS, ELEM), 1)), 1.0, 0.0)
    far_ref[...] = jnp.concatenate([came, jnp.zeros((64, ELEM), F32)], axis=0).T[:, :ROWS].astype(BF16)
    sum_ref[...] = select_nt(near.T.astype(BF16), donor_ref[...])
    for v in range(VARS):
        wide_ref[0:NODES, :] = sec_ref[v]
        wide_ref[NODES:128, :] = jnp.zeros((3, ELEM), F32)
        value = wide_ref[...].T
        mean = jnp.broadcast_to(mean_ref[v : v + 1, :], (ELEM, ELEM)).T
        still_ref[:, 128 * v : 128 * v + 128] = jnp.where(troubled > 0.5, mean, value)
    owner = owner_ref[...]
    out0 = jnp.where(odd == 1, left, right)
    out1 = jnp.where(odd == 1, right, left)
    stays = jnp.where(owner == own, 1.0, 0.0)
    cell_ref[:, 0:128] = jnp.broadcast_to(troubled, (ELEM, ELEM))
    cell_ref[:, 128:256] = jnp.broadcast_to(stays, (ELEM, ELEM)).T
    go0 = jnp.where(owner == out0, 1.0, 0.0)
    go1 = jnp.where(owner == out1, 1.0, 0.0)
    go = jnp.concatenate([go0, go1, jnp.zeros((6, ELEM), F32)], axis=0)
    order = dot_nn(go.astype(BF16), strict_upper())
    place = jnp.where(go0 > 0.5, order[0:1, :], jnp.where(go1 > 0.5, MOVE_CAP + order[1:2, :], -1.0))
    move_ref[...] = onehot(iota((2 * MOVE_CAP, ELEM), 0) == place.astype(I32))


def limit_kernel(
    grp_ref, pair0_ref, pair1_ref, sum_ref, still_ref, far_ref, move_ref, cell_ref,
    limited_ref, go0_ref, go1_ref,
):
    got = jnp.concatenate([grp_ref[...], pair0_ref[...], pair1_ref[...]], axis=0)
    hi, mid = halves(got)
    far = far_ref[...]
    total = sum_ref[...] + (dot_nn(far, hi) + dot_nn(far, mid))
    troubled = cell_ref[:, 0:1] > 0.5
    for v in range(VARS):
        cols = slice(128 * v, 128 * v + 128)
        scale = jnp.where(troubled, 1.0 / total[:, 128 * v + NODES : 128 * v + NODES + 1], 0.0)
        limited_ref[:, cols] = still_ref[:, cols] + scale * total[:, cols]
    hi, mid, lo = thirds(limited_ref[...])
    move = move_ref[...]
    moved = dot_nn(move, hi) + dot_nn(move, mid) + dot_nn(move, lo)
    for v in range(VARS):
        go0_ref[v] = moved[:MOVE_CAP, 128 * v : 128 * v + NODES]
        go1_ref[v] = moved[MOVE_CAP:, 128 * v : 128 * v + NODES]


def keep_kernel(limited_ref, cell_ref, out_ref):
    stays = cell_ref[:, 128:256] > 0.5
    for v in range(VARS):
        out_ref[v] = jnp.where(stays, limited_ref[:, 128 * v : 128 * v + 128], 0.0)[:, :NODES]


def arrive_kernel(in0_ref, in1_ref, kept_ref, out_ref, sems):
    odd = lax.rem(lax.axis_index("wide"), 2)
    copies = []
    for k, (ref, place) in enumerate(((in0_ref, 1 - odd), (in1_ref, odd))):
        at = pl.ds(pl.multiple_of(ELEM + MOVE_CAP * place, 32), MOVE_CAP)
        copies.append(pltpu.make_async_copy(ref, out_ref.at[:, at, :], sems.at[k]))
    for copy in copies:
        copy.start()
    for copy in copies:
        copy.wait()


VMEM = pl.BlockSpec(memory_space=pltpu.VMEM)
PARAMS = pltpu.CompilerParams(vmem_limit_bytes=16 * 1024 * 1024)


def call(kernel, shapes, scratch, args, hbm=(), to_hbm=0):
    inputs = [pltpu.with_memory_space_constraint(arg, pltpu.VMEM) for arg in args]
    inputs += [pltpu.with_memory_space_constraint(arg, pltpu.HBM) for arg in hbm]
    spaces = [pltpu.HBM] * to_hbm + [pltpu.VMEM] * (len(shapes) - to_hbm)
    return pl.pallas_call(
        kernel,
        out_shape=[space(shape, dtype) for space, (shape, dtype) in zip(spaces, shapes)],
        in_specs=[VMEM] * len(args) + [pl.BlockSpec(memory_space=pltpu.HBM)] * len(hbm),
        out_specs=[pl.BlockSpec(memory_space=space) for space in spaces],
        scratch_shapes=scratch,
        compiler_params=PARAMS,
        interpret=INTERPRET,
    )(*inputs)


def swap(pair0, pair1):
    size = lax.axis_size("wide")
    first = [(i, i ^ 1) for i in range(size)]
    second = [(i, (i + 1) % size if i % 2 else (i - 1) % size) for i in range(size)]
    got1 = lax.ppermute(pair1, "wide", second)
    got0 = lax.ppermute(pair0, "wide", first)
    return got0, got1


def exchange(blocks, pair0, pair1):
    lanes = blocks.shape[1]
    got = lax.all_to_all(blocks.reshape(GROUP, GROUP_FACES, lanes), "grp", 0, 0)
    return (got.reshape(GROUP_ROWS, lanes), *swap(pair0, pair1))


def shards(state, metric, nbr_elem, nbr_face, troubled, new_owner):
    diffs, weights = gll_tables()
    diff = np.zeros((128, 384), np.float32)
    for a in range(3):
        diff[:NODES, 128 * a : 128 * a + NODES] = diffs[a]
    diff = jnp.asarray(np.concatenate(halves_of(diff), axis=0))
    weight = jnp.asarray(np.repeat(weights[:, None], ELEM, axis=1), F32)
    metric = metric.reshape(1, ELEM)
    troubled = troubled.reshape(1, 48)
    new_owner = new_owner.reshape(1, ELEM)
    cols = VARS * 128
    slots = FACES * ELEM
    dma = pltpu.SemaphoreType.DMA

    loaded = (nbr_elem, nbr_face, state, metric, troubled, new_owner, diff, weight)
    results = call(
        pack_kernel,
        [((GROUP_ROWS, 128), F32), ((32, 128), F32), ((32, 128), F32), ((128, slots), F32), ((ROWS, ELEM), BF16),
         ((VARS, NODES, ELEM), F32)]
        + [(x.shape, x.dtype) for x in (nbr_elem, nbr_face, metric, troubled, new_owner, weight)],
        [pltpu.VMEM(state.shape, F32), pltpu.VMEM(diff.shape, BF16), pltpu.VMEM((ROWS, slots), BF16),
         pltpu.VMEM((GROUP_ROWS, 128), F32), pltpu.VMEM((384, cols), F32), dma((8 + VARS,))],
        (), loaded, 1,
    )
    blocks, pair0, pair1, trace, pick, start = results[:6]
    nbr_elem, nbr_face, metric, troubled, new_owner, weight = results[6:]
    got, got0, got1 = exchange(blocks, pair0, pair1)
    base, speeds, near = call(
        local_kernel,
        [((VARS, NODES, ELEM), F32), ((FACES, 25, ELEM), F32), ((128, slots), F32)],
        [],
        (nbr_elem, nbr_face, start, metric, trace),
    )
    blocks, pair0, pair1, sec, donor, mean, came = call(
        section_kernel,
        [((GROUP_ROWS, cols), F32), ((32, cols), F32), ((32, cols), F32), ((VARS, NODES, ELEM), F32),
         ((cols, ELEM), F32), ((8, ELEM), F32), ((ROWS, ELEM), F32)],
        [pltpu.VMEM((128, slots), F32), pltpu.VMEM((GROUP_ROWS, cols), F32), dma((1,))],
        (got, got0, got1, base, speeds, near, trace, pick, metric, weight), (), 1,
    )
    got, got0, got1 = exchange(blocks, pair0, pair1)
    total, still, far, move, cell = call(
        inside_kernel,
        [((ELEM, cols), F32), ((ELEM, cols), F32), ((ELEM, ROWS), BF16), ((2 * MOVE_CAP, ELEM), BF16), ((ELEM, 256), F32)],
        [pltpu.VMEM((128, ELEM), F32)],
        (nbr_elem, troubled, new_owner, came, donor, mean, sec),
    )
    limited, go0, go1 = call(
        limit_kernel,
        [((ELEM, cols), F32), ((VARS, MOVE_CAP, NODES), F32), ((VARS, MOVE_CAP, NODES), F32)],
        [],
        (got, got0, got1, total, still, far, move, cell),
    )
    in0, in1 = swap(go0, go1)
    out_shape = jax.ShapeDtypeStruct((VARS, ELEM + 2 * MOVE_CAP, NODES), F32)
    vmem = lambda x: pltpu.with_memory_space_constraint(x, pltpu.VMEM)
    kept = pl.pallas_call(
        keep_kernel,
        out_shape=out_shape,
        grid=(1,),
        in_specs=[VMEM, VMEM],
        out_specs=pl.BlockSpec((VARS, ELEM, NODES), lambda i: (0, 0, 0)),
        compiler_params=PARAMS,
        interpret=INTERPRET,
    )(vmem(limited), vmem(cell))
    moved = pl.pallas_call(
        arrive_kernel,
        out_shape=out_shape,
        in_specs=[VMEM, VMEM, pl.BlockSpec(memory_space=pl.ANY)],
        out_specs=pl.BlockSpec(memory_space=pl.ANY),
        input_output_aliases={2: 0},
        scratch_shapes=[dma((2,))],
        compiler_params=PARAMS,
        interpret=INTERPRET,
    )(vmem(in0), vmem(in1), kept)
    return jnp.transpose(moved, (0, 2, 1))


def solution(mesh):
    placed = (
        P(None, None, ("wide", "grp")),
        P(("wide", "grp")),
        P(None, ("wide", "grp")),
        P(None, ("wide", "grp")),
        P(("wide", "grp")),
        P(("wide", "grp")),
    )
    return jax.shard_map(
        shards,
        mesh=mesh,
        in_specs=placed,
        out_specs=P(None, None, ("wide", "grp")),
        check_vma=False,
    )
```

```python
import math

import jax
import jax.numpy as jnp
import numpy as np
from jax import lax
from jax.experimental import pallas as pl
from jax.experimental.pallas import tpu as pltpu
from jax.sharding import PartitionSpec as P


GROUP_FACES = 16
WIDE_FACES = 32
MOVE_CAP = 32
SECTION_STEP = 0.01
LIFT_GAIN = 10.0

ELEM = 128
VARS = 5
NODES = 125
FACES = 6
GROUP = 8
GROUP_ROWS = GROUP * GROUP_FACES
PAIR1 = GROUP_ROWS + WIDE_FACES
ROWS = GROUP_ROWS + 2 * WIDE_FACES
LOCAL = 10
HALF = GROUP_ROWS // 2
TURN_A = False
TURN_B = True

F32 = jnp.float32
BF16 = jnp.bfloat16
I32 = jnp.int32
INTERPRET = False


def gll_tables():
    root = math.sqrt(3.0 / 7.0)
    points = np.array([-1.0, -root, 0.0, root, 1.0])
    weights = np.array([0.1, 49.0 / 90.0, 32.0 / 45.0, 49.0 / 90.0, 0.1])
    bary = np.array(
        [1.0 / np.prod([points[j] - points[k] for k in range(5) if k != j]) for j in range(5)]
    )
    deriv = np.zeros((5, 5))
    for i in range(5):
        for j in range(5):
            if i != j:
                deriv[i, j] = bary[j] / bary[i] / (points[i] - points[j])
        deriv[i, i] = -np.sum(deriv[i])
    ident = np.eye(5)
    diffs = [
        np.kron(np.kron(deriv, ident), ident),
        np.kron(np.kron(ident, deriv), ident),
        np.kron(np.kron(ident, ident), deriv),
    ]
    cell_weights = np.kron(np.kron(weights, weights), weights) / 8.0
    return diffs, cell_weights


def halves_of(table):
    hi = table.astype(jnp.bfloat16)
    return hi, (table - hi.astype(np.float32)).astype(jnp.bfloat16)


def face_rows(face):
    if face < 2:
        return [(100 * face, 25, 1, 0)]
    if face < 4:
        return [(25 * a + 20 * (face - 2), 5, 1, 5 * a) for a in range(5)]
    return [(4 * (face - 4), 25, 5, 0)]


def rows_at(first, count, stride):
    return pl.ds(first, count) if stride == 1 else pl.ds(first, count, stride=stride)


def thirds(x):
    hi = x.astype(BF16)
    rest = x - hi.astype(F32)
    mid = rest.astype(BF16)
    lo = (rest - mid.astype(F32)).astype(BF16)
    return hi, mid, lo


def halves(x):
    hi = x.astype(BF16)
    return hi, (x - hi.astype(F32)).astype(BF16)


def dot_nn(a, b):
    return lax.dot_general(a, b, (((1,), (0,)), ((), ())), preferred_element_type=F32)


def dot_nt(a, b):
    return lax.dot_general(a, b, (((1,), (1,)), ((), ())), preferred_element_type=F32)


def select_nt(onehot, values):
    hi, mid, lo = thirds(values)
    return dot_nt(onehot, hi) + dot_nt(onehot, mid) + dot_nt(onehot, lo)


def turned(rows, turn):
    return jnp.concatenate([rows[HALF:], rows[:HALF]], axis=0) if turn else rows


def iota(shape, dim):
    return lax.broadcasted_iota(I32, shape, dim)


def onehot(mask):
    return jnp.where(mask, 1.0, 0.0).astype(BF16)


def places():
    wide = lax.axis_index("wide")
    grp = lax.axis_index("grp")
    size = lax.axis_size("wide")
    left = lax.rem(wide + size - 1, size) * GROUP + grp
    right = lax.rem(wide + 1, size) * GROUP + grp
    odd = lax.rem(wide, 2)
    return wide, grp, left, right, odd


def categories(nbr_elem):
    wide, grp, left, _, odd = places()
    owner = lax.shift_right_logical(nbr_elem, 7)
    beside = jnp.where(owner == left, 9 - odd, 8 + odd)
    cat = jnp.where(lax.shift_right_logical(owner, 3) == wide, owner & 7, beside)
    return jnp.where(owner == wide * GROUP + grp, LOCAL, cat)


def strict_upper():
    return onehot(iota((ELEM, ELEM), 0) < iota((ELEM, ELEM), 1))


def pack_kernel(
    elem_hbm, face_hbm, state_hbm, metric_hbm, troubled_hbm, owner_hbm, diff_hbm, weight_hbm,
    grp_hbm, pair0_ref, pair1_ref, trace_ref, pick_ref, base_ref,
    elem_ref, face_ref, metric_ref, troubled_ref, owner_ref, weight_ref,
    state_ref, diff_ref, s_ref, grp_ref, f_ref, sems,
):
    pairs = [(elem_hbm, elem_ref), (face_hbm, face_ref)]
    pairs += [(state_hbm.at[v], state_ref.at[v]) for v in range(VARS)]
    pairs += [(metric_hbm, metric_ref), (troubled_hbm, troubled_ref), (owner_hbm, owner_ref)]
    pairs += [(diff_hbm, diff_ref), (weight_hbm, weight_ref)]
    copies = [pltpu.make_async_copy(x, y, sems.at[k]) for k, (x, y) in enumerate(pairs)]
    for copy in copies:
        copy.start()
    copies[0].wait()
    copies[1].wait()
    elem = elem_ref[...]
    cat = categories(elem)
    partner = face_ref[...] * ELEM + (elem & (ELEM - 1)) + 1
    kinds = iota((16, ELEM), 0)
    hot = [jnp.where(cat[f : f + 1, :] == kinds, 1.0, 0.0) for f in range(FACES)]
    upper = jnp.concatenate([strict_upper(), jnp.ones((ELEM, ELEM), BF16)], axis=1)
    counts = dot_nn(jnp.concatenate(hot, axis=0).astype(BF16), upper)
    base = jnp.where(kinds < 9, 16 * kinds, PAIR1).astype(F32)
    pick = jnp.zeros((ROWS, ELEM), F32)
    rows = iota((ROWS, ELEM), 0)
    trace_ref[126:128, :] = jnp.zeros((2, FACES * ELEM), F32)
    for f in range(FACES):
        part = counts[16 * f : 16 * f + 16]
        pos = jnp.sum(hot[f] * (part[:, :ELEM] + base), axis=0, keepdims=True)
        base = base + part[:, ELEM:]
        pos = jnp.where(cat[f : f + 1, :] == LOCAL, -1, pos.astype(I32))
        chosen = jnp.where(rows == pos, 1.0, 0.0)
        pick = pick + chosen
        s_ref[:, f * ELEM : (f + 1) * ELEM] = chosen.astype(BF16)
        trace_ref[125:126, f * ELEM : (f + 1) * ELEM] = partner[f : f + 1, :].astype(F32)
    pick_ref[...] = pick.astype(BF16)
    for v in range(VARS):
        copies[2 + v].wait()
        for f in range(FACES):
            for first, count, stride, place in face_rows(f):
                trace_ref[25 * v + place : 25 * v + place + count, f * ELEM : (f + 1) * ELEM] = state_ref[
                    v, rows_at(first, count, stride), :
                ]
    pieces = halves(trace_ref[...])
    grp_ref[...] = turned(sum(dot_nt(s_ref[:GROUP_ROWS], x) for x in pieces), TURN_A)
    send = pltpu.make_async_copy(grp_ref, grp_hbm, sems.at[len(copies)])
    send.start()
    sent = sum(dot_nt(s_ref[GROUP_ROWS:], x) for x in pieces)
    pair0_ref[...] = sent[:WIDE_FACES]
    pair1_ref[...] = sent[WIDE_FACES:]
    u = [state_ref[v] for v in range(VARS)]
    _, vel, pressure = primitives(u)
    for a in range(3):
        for v, row in enumerate(flux(u, vel, pressure, a)):
            f_ref[128 * a : 128 * a + NODES, v * ELEM : (v + 1) * ELEM] = row
        f_ref[128 * a + NODES : 128 * a + 128, :] = jnp.zeros((3, VARS * ELEM), F32)
    hi, mid = halves(f_ref[...])
    for copy in copies[2 + VARS :]:
        copy.wait()
    wide = dot_nn(diff_ref[...], hi)
    volume = wide[:128] + wide[128:] + dot_nn(diff_ref[0:128, :], mid)
    step = SECTION_STEP * metric_ref[...]
    for v in range(VARS):
        base_ref[v] = state_ref[v] - step * volume[:NODES, v * ELEM : (v + 1) * ELEM]
    send.wait()


def primitives(u):
    inv = 1.0 / u[0]
    vel = [u[1] * inv, u[2] * inv, u[3] * inv]
    kinetic = u[1] * vel[0] + u[2] * vel[1] + u[3] * vel[2]
    pressure = 0.4 * (u[4] - 0.5 * kinetic)
    return inv, vel, pressure


def flux(u, vel, pressure, a):
    w = vel[a]
    rows = [u[1 + a], u[1] * w, u[2] * w, u[3] * w, (u[4] + pressure) * w]
    rows[1 + a] = rows[1 + a] + pressure
    return rows


def speed(inv, vel, pressure, a):
    return jnp.abs(vel[a]) + jnp.sqrt(1.4 * pressure * inv)


def face_values(ref, f):
    return [ref[25 * v : 25 * v + 25, f * ELEM : (f + 1) * ELEM] for v in range(VARS)]


def add_face(ref, f, v, value):
    for first, count, stride, place in face_rows(f):
        at = rows_at(first, count, stride)
        ref[v, at, :] = ref[v, at, :] + value[place : place + count]


def local_kernel(
    elem_ref, face_ref, start_ref, metric_ref, trace_ref,
    base_ref, speed_ref, near_ref,
):
    metric = metric_ref[...]
    for v in range(VARS):
        base_ref[v] = start_ref[v]
    elem = elem_ref[...]
    _, grp, _, _, _ = places()
    own = lax.axis_index("wide") * GROUP + grp
    here = lax.shift_right_logical(elem, 7) == own
    local = elem & (ELEM - 1)
    side = face_ref[...]
    at = [jnp.where(here & (side == g), local, -1).astype(F32).astype(BF16) for g in range(FACES)]
    elems = iota((ELEM, 2 * ELEM), 0).astype(F32).astype(BF16)
    one, zero = jnp.ones((), BF16), jnp.zeros((), BF16)
    stacked = jnp.concatenate(halves(trace_ref[...]), axis=0)
    half = (0.5 * LIFT_GAIN * SECTION_STEP) * metric
    for pair in range(3):
        blocks = []
        for g in range(FACES):
            row = jnp.concatenate([at[g][2 * pair : 2 * pair + 1], at[g][2 * pair + 1 : 2 * pair + 2]], axis=1)
            blocks.append(jnp.where(elems == row, one, zero))
        got = dot_nn(stacked, jnp.concatenate(blocks, axis=0))
        near_ref[:, 2 * pair * ELEM : 2 * (pair + 1) * ELEM] = got[:128] + got[128:]
        for f in (2 * pair, 2 * pair + 1):
            scale = half if f % 2 else -half
            inner = face_values(trace_ref, f)
            inv, vel, pressure = primitives(inner)
            speed_ref[f] = speed(inv, vel, pressure, pair)
            for v, row in enumerate(flux(inner, vel, pressure, pair)):
                add_face(base_ref, f, v, scale * row)


def section_kernel(
    grp_ref, pair0_ref, pair1_ref, base_ref, speed_ref, near_ref, trace_ref, pick_ref, metric_ref, weight_ref,
    send_hbm, send0_ref, send1_ref, sec_ref, donor_ref, mean_ref, came_ref, outer_ref, send_ref, sem,
):
    got = jnp.concatenate([turned(grp_ref[...], TURN_A), pair0_ref[...], pair1_ref[...]], axis=0)
    slot = jnp.broadcast_to(got[:, NODES : NODES + 1], (ROWS, ELEM))
    lanes = iota((1, ELEM), 1).astype(F32) + 1.0
    stacked = jnp.concatenate(halves(got.T), axis=0)
    for pair in range(3):
        takes = [jnp.where(slot == lanes + float(f * ELEM), 1.0, 0.0) for f in (2 * pair, 2 * pair + 1)]
        far = dot_nn(stacked, jnp.concatenate(takes, axis=1).astype(BF16))
        cols = slice(2 * pair * ELEM, 2 * (pair + 1) * ELEM)
        outer_ref[:, cols] = near_ref[:, cols] + far[:128] + far[128:]
    came_ref[...] = slot
    half = (0.5 * LIFT_GAIN * SECTION_STEP) * metric_ref[...]
    sec_ref[...] = base_ref[...]
    for f in range(FACES):
        a = f // 2
        sign = 1.0 if f % 2 else -1.0
        inner = face_values(trace_ref, f)
        outer = face_values(outer_ref, f)
        inv, vel, pressure = primitives(outer)
        lam = half * jnp.maximum(speed_ref[f], speed(inv, vel, pressure, a))
        for v, row in enumerate(flux(outer, vel, pressure, a)):
            add_face(sec_ref, f, v, lam * (outer[v] - inner[v]) - (sign * half) * row)
    weight = weight_ref[...]
    for v in range(VARS):
        q = sec_ref[v]
        mean = jnp.sum(weight * q, axis=0, keepdims=True)
        dev = q - mean
        beta = 1e-06 + jnp.sum(weight * dev * dev, axis=0, keepdims=True)
        omega = 0.1 / (beta * beta)
        donor_ref[128 * v : 128 * v + NODES, :] = omega * dev
        donor_ref[128 * v + NODES : 128 * v + NODES + 1, :] = omega
        donor_ref[128 * v + NODES + 1 : 128 * v + 128, :] = jnp.zeros((2, ELEM), F32)
        mean_ref[v : v + 1, :] = mean
    pieces = halves(donor_ref[...])
    send_ref[...] = turned(sum(dot_nt(pick_ref[:GROUP_ROWS], x) for x in pieces), TURN_B)
    send = pltpu.make_async_copy(send_ref, send_hbm, sem.at[0])
    send.start()
    sent = sum(dot_nt(pick_ref[GROUP_ROWS:], x) for x in pieces)
    send0_ref[...] = sent[:WIDE_FACES]
    send1_ref[...] = sent[WIDE_FACES:]
    send.wait()


def inside_kernel(
    elem_ref, troubled_ref, owner_ref, came_ref, donor_ref, mean_ref, sec_ref,
    sum_ref, still_ref, far_ref, move_ref, cell_ref, wide_ref,
):
    _, grp, left, right, odd = places()
    own = lax.axis_index("wide") * GROUP + grp
    elem = elem_ref[...]
    troubled = jnp.sum(
        jnp.where(troubled_ref[...] == iota((ELEM, 48), 0), 1.0, 0.0), axis=1, keepdims=True
    )
    local = jnp.where(lax.shift_right_logical(elem, 7) == own, elem & (ELEM - 1), -1)
    elems = iota((ELEM, ELEM), 0)
    near = jnp.where(elems == iota((ELEM, ELEM), 1), 4.0, 0.0)
    for f in range(FACES):
        near = near + jnp.where(elems == local[f : f + 1, :], 1.0, 0.0)
    slot = came_ref[...].astype(I32) - 1
    came = jnp.where((slot & (ELEM - 1)) == jnp.where(slot < 0, -1, iota((ROWS, ELEM), 1)), 1.0, 0.0)
    far_ref[...] = jnp.concatenate([came, jnp.zeros((64, ELEM), F32)], axis=0).T[:, :ROWS].astype(BF16)
    sum_ref[...] = select_nt(near.T.astype(BF16), donor_ref[...])
    for v in range(VARS):
        wide_ref[0:NODES, :] = sec_ref[v]
        wide_ref[NODES:128, :] = jnp.zeros((3, ELEM), F32)
        value = wide_ref[...].T
        mean = jnp.broadcast_to(mean_ref[v : v + 1, :], (ELEM, ELEM)).T
        still_ref[:, 128 * v : 128 * v + 128] = jnp.where(troubled > 0.5, mean, value)
    owner = owner_ref[...]
    out0 = jnp.where(odd == 1, left, right)
    out1 = jnp.where(odd == 1, right, left)
    stays = jnp.where(owner == own, 1.0, 0.0)
    cell_ref[:, 0:128] = jnp.broadcast_to(troubled, (ELEM, ELEM))
    cell_ref[:, 128:256] = jnp.broadcast_to(stays, (ELEM, ELEM)).T
    go0 = jnp.where(owner == out0, 1.0, 0.0)
    go1 = jnp.where(owner == out1, 1.0, 0.0)
    go = jnp.concatenate([go0, go1, jnp.zeros((6, ELEM), F32)], axis=0)
    order = dot_nn(go.astype(BF16), strict_upper())
    place = jnp.where(go0 > 0.5, order[0:1, :], jnp.where(go1 > 0.5, MOVE_CAP + order[1:2, :], -1.0))
    move_ref[...] = onehot(iota((2 * MOVE_CAP, ELEM), 0) == place.astype(I32))


def limit_kernel(
    grp_ref, pair0_ref, pair1_ref, sum_ref, still_ref, far_ref, move_ref, cell_ref,
    limited_ref, go0_ref, go1_ref,
):
    got = jnp.concatenate([turned(grp_ref[...], TURN_B), pair0_ref[...], pair1_ref[...]], axis=0)
    hi, mid = halves(got)
    far = far_ref[...]
    total = sum_ref[...] + (dot_nn(far, hi) + dot_nn(far, mid))
    troubled = cell_ref[:, 0:1] > 0.5
    for v in range(VARS):
        cols = slice(128 * v, 128 * v + 128)
        scale = jnp.where(troubled, 1.0 / total[:, 128 * v + NODES : 128 * v + NODES + 1], 0.0)
        limited_ref[:, cols] = still_ref[:, cols] + scale * total[:, cols]
    hi, mid, lo = thirds(limited_ref[...])
    move = move_ref[...]
    moved = dot_nn(move, hi) + dot_nn(move, mid) + dot_nn(move, lo)
    for v in range(VARS):
        go0_ref[v] = moved[:MOVE_CAP, 128 * v : 128 * v + NODES]
        go1_ref[v] = moved[MOVE_CAP:, 128 * v : 128 * v + NODES]


def keep_kernel(limited_ref, cell_ref, out_ref):
    stays = cell_ref[:, 128:256] > 0.5
    for v in range(VARS):
        out_ref[v] = jnp.where(stays, limited_ref[:, 128 * v : 128 * v + 128], 0.0)[:, :NODES]


def arrive_kernel(in0_ref, in1_ref, kept_ref, out_ref, sems):
    odd = lax.rem(lax.axis_index("wide"), 2)
    copies = []
    for k, (ref, place) in enumerate(((in0_ref, 1 - odd), (in1_ref, odd))):
        at = pl.ds(pl.multiple_of(ELEM + MOVE_CAP * place, 32), MOVE_CAP)
        copies.append(pltpu.make_async_copy(ref, out_ref.at[:, at, :], sems.at[k]))
    for copy in copies:
        copy.start()
    for copy in copies:
        copy.wait()


VMEM = pl.BlockSpec(memory_space=pltpu.VMEM)
PARAMS = pltpu.CompilerParams(vmem_limit_bytes=16 * 1024 * 1024)


def call(kernel, shapes, scratch, args, hbm=(), to_hbm=0):
    inputs = [pltpu.with_memory_space_constraint(arg, pltpu.VMEM) for arg in args]
    inputs += [pltpu.with_memory_space_constraint(arg, pltpu.HBM) for arg in hbm]
    spaces = [pltpu.HBM] * to_hbm + [pltpu.VMEM] * (len(shapes) - to_hbm)
    return pl.pallas_call(
        kernel,
        out_shape=[space(shape, dtype) for space, (shape, dtype) in zip(spaces, shapes)],
        in_specs=[VMEM] * len(args) + [pl.BlockSpec(memory_space=pltpu.HBM)] * len(hbm),
        out_specs=[pl.BlockSpec(memory_space=space) for space in spaces],
        scratch_shapes=scratch,
        compiler_params=PARAMS,
        interpret=INTERPRET,
    )(*inputs)


def swap(pair0, pair1):
    size = lax.axis_size("wide")
    first = [(i, i ^ 1) for i in range(size)]
    second = [(i, (i + 1) % size if i % 2 else (i - 1) % size) for i in range(size)]
    got1 = lax.ppermute(pair1, "wide", second)
    got0 = lax.ppermute(pair0, "wide", first)
    return got0, got1


def exchange(blocks, pair0, pair1, turn):
    order = [[4, 5, 6, 7, 0, 1, 2, 3]] if turn else None
    lanes = blocks.shape[1]
    got = lax.all_to_all(
        blocks.reshape(GROUP, GROUP_FACES, lanes), "grp", 0, 0, axis_index_groups=order
    )
    return (got.reshape(GROUP_ROWS, lanes), *swap(pair0, pair1))


def shards(state, metric, nbr_elem, nbr_face, troubled, new_owner):
    diffs, weights = gll_tables()
    diff = np.zeros((128, 384), np.float32)
    for a in range(3):
        diff[:NODES, 128 * a : 128 * a + NODES] = diffs[a]
    diff = jnp.asarray(np.concatenate(halves_of(diff), axis=0))
    weight = jnp.asarray(np.repeat(weights[:, None], ELEM, axis=1), F32)
    metric = metric.reshape(1, ELEM)
    troubled = troubled.reshape(1, 48)
    new_owner = new_owner.reshape(1, ELEM)
    cols = VARS * 128
    slots = FACES * ELEM
    dma = pltpu.SemaphoreType.DMA

    loaded = (nbr_elem, nbr_face, state, metric, troubled, new_owner, diff, weight)
    results = call(
        pack_kernel,
        [((GROUP_ROWS, 128), F32), ((32, 128), F32), ((32, 128), F32), ((128, slots), F32), ((ROWS, ELEM), BF16),
         ((VARS, NODES, ELEM), F32)]
        + [(x.shape, x.dtype) for x in (nbr_elem, nbr_face, metric, troubled, new_owner, weight)],
        [pltpu.VMEM(state.shape, F32), pltpu.VMEM(diff.shape, BF16), pltpu.VMEM((ROWS, slots), BF16),
         pltpu.VMEM((GROUP_ROWS, 128), F32), pltpu.VMEM((384, cols), F32), dma((8 + VARS,))],
        (), loaded, 1,
    )
    blocks, pair0, pair1, trace, pick, start = results[:6]
    nbr_elem, nbr_face, metric, troubled, new_owner, weight = results[6:]
    got, got0, got1 = exchange(blocks, pair0, pair1, TURN_A)
    base, speeds, near = call(
        local_kernel,
        [((VARS, NODES, ELEM), F32), ((FACES, 25, ELEM), F32), ((128, slots), F32)],
        [],
        (nbr_elem, nbr_face, start, metric, trace),
    )
    blocks, pair0, pair1, sec, donor, mean, came = call(
        section_kernel,
        [((GROUP_ROWS, cols), F32), ((32, cols), F32), ((32, cols), F32), ((VARS, NODES, ELEM), F32),
         ((cols, ELEM), F32), ((8, ELEM), F32), ((ROWS, ELEM), F32)],
        [pltpu.VMEM((128, slots), F32), pltpu.VMEM((GROUP_ROWS, cols), F32), dma((1,))],
        (got, got0, got1, base, speeds, near, trace, pick, metric, weight), (), 1,
    )
    got, got0, got1 = exchange(blocks, pair0, pair1, TURN_B)
    total, still, far, move, cell = call(
        inside_kernel,
        [((ELEM, cols), F32), ((ELEM, cols), F32), ((ELEM, ROWS), BF16), ((2 * MOVE_CAP, ELEM), BF16), ((ELEM, 256), F32)],
        [pltpu.VMEM((128, ELEM), F32)],
        (nbr_elem, troubled, new_owner, came, donor, mean, sec),
    )
    limited, go0, go1 = call(
        limit_kernel,
        [((ELEM, cols), F32), ((VARS, MOVE_CAP, NODES), F32), ((VARS, MOVE_CAP, NODES), F32)],
        [],
        (got, got0, got1, total, still, far, move, cell),
    )
    in0, in1 = swap(go0, go1)
    out_shape = jax.ShapeDtypeStruct((VARS, ELEM + 2 * MOVE_CAP, NODES), F32)
    vmem = lambda x: pltpu.with_memory_space_constraint(x, pltpu.VMEM)
    kept = pl.pallas_call(
        keep_kernel,
        out_shape=out_shape,
        grid=(1,),
        in_specs=[VMEM, VMEM],
        out_specs=pl.BlockSpec((VARS, ELEM, NODES), lambda i: (0, 0, 0)),
        compiler_params=PARAMS,
        interpret=INTERPRET,
    )(vmem(limited), vmem(cell))
    moved = pl.pallas_call(
        arrive_kernel,
        out_shape=out_shape,
        in_specs=[VMEM, VMEM, pl.BlockSpec(memory_space=pl.ANY)],
        out_specs=pl.BlockSpec(memory_space=pl.ANY),
        input_output_aliases={2: 0},
        scratch_shapes=[dma((2,))],
        compiler_params=PARAMS,
        interpret=INTERPRET,
    )(vmem(in0), vmem(in1), kept)
    return jnp.transpose(moved, (0, 2, 1))


def solution(mesh):
    placed = (
        P(None, None, ("wide", "grp")),
        P(("wide", "grp")),
        P(None, ("wide", "grp")),
        P(None, ("wide", "grp")),
        P(("wide", "grp")),
        P(("wide", "grp")),
    )
    return jax.shard_map(
        shards,
        mesh=mesh,
        in_specs=placed,
        out_specs=P(None, None, ("wide", "grp")),
        check_vma=False,
    )
```
